256 devices in a mesh: view: 2 (over x_hi), seq: 8 (over y, core), event: 16 (over x_lo, z).
Axes of the slice: x: 4 (x_hi: 2, x_lo: 2; x = x_hi * 2 + x_lo), y: 4, z: 8, core: 2. Of those that a mesh axis runs over, the one named last changes fastest.
Arguments:
- query: bfloat16 [16, 2, 3072, 512], P('event', 'view', 'seq'), may hold values from -7 to 7
- key: bfloat16 [16, 2, 3072, 512], P('event', 'view', 'seq'), may hold values from -7 to 7
- value: bfloat16 [16, 2, 3072, 512], P('event', 'view', 'seq'), may hold values from -6 to 6
- pattern: int32 [16, 2, 24, 24], P('event', 'view', 'seq'), may hold values from 0 to 1, as said below
- out_weight: bfloat16 [512, 512], replicated, may hold values from -0.25 to 0.25
- served: int32 [16, 2, 128, 128], P('event', 'view', 'seq'), may hold values from 0 to 383
- anchor_rows: int32 [16, 2, 2048], P('event', 'view', 'seq'), may hold values from 0 to 383
- positive_slot: int32 [16, 2, 2048], P('event', 'view', 'seq'), may hold values from 0 to 2047, as said below
- anchor_live: int32 [16, 2, 2048], P('event', 'view', 'seq'), may hold values from 0 to 1, as said below
Outputs:
- mixed: bfloat16 [16, 2, 3072, 512], P('event', 'view', 'seq')
- grad_wo: float32 [512, 512], replicated
- loss: float32 [], replicated
The draws below stay inside these ranges and needn't reach their ends.
Inputs may be any that keep to these rules, and one draw needn't show every extreme that they name: pattern[e, v, b, b] is 1 for every block b. `positive_slot`: for an anchor of view v the slot lies in [(1 - v) * 1024, (2 - v) * 1024), a point of the other view. `anchor_live`: every device's block of 256 anchors holds at least one live anchor.
All inputs are finite; a program needn't handle non-finite values.
Results may differ from the reference program's by a relative error of at most 0.015.
Values may be sent and summed in bfloat16 or wider, within the bound.
No kernel may reach another device: no remote copies, remote signals or barrier semaphores. Data moves between devices by JAX's collectives and lax.ppermute only.
A program may use at most 64 MiB of HBM per device.

```python
import jax
import jax.numpy as jnp
from jax import lax

D = 512
HEADS = 16
BLOCK = 128
PTS_DEV = 384
CAP = 128
PAIRS_DEV = 256
EVENTS = 16
NPTS = 3072
NB = 24
REQS = 128
CANDS = 2048
PAIRS = 2048
N_SEQ = 8


def draw_query(key, part):
    shape = (EVENTS, 2, NPTS, D)
    base = jnp.clip(1.5 * jax.random.normal(jax.random.fold_in(key, 1), shape, jnp.float32), -7.0, 7.0)
    return base.astype(jnp.bfloat16)


def draw_key(key, part):
    shape = (EVENTS, 2, NPTS, D)
    base = jnp.clip(1.5 * jax.random.normal(jax.random.fold_in(key, 2), shape, jnp.float32), -7.0, 7.0)
    return base.astype(jnp.bfloat16)


def draw_pattern(key, part):
    level = jax.random.randint(jax.random.fold_in(key, 7), (EVENTS, 2, NB, 1), 1, 9)
    rolled = jax.random.randint(jax.random.fold_in(key, 8), (EVENTS, 2, NB, NB), 0, 16)
    diagonal = jnp.arange(NB)[:, None] == jnp.arange(NB)[None, :]
    return jnp.where((rolled < level) | diagonal[None, None], 1, 0).astype(jnp.int32)


def draw_positive_slot(key, part):
    half = CANDS // 2
    offset = jax.random.randint(jax.random.fold_in(key, 41), (EVENTS, 2, PAIRS), 0, half)
    side = jnp.arange(2, dtype=jnp.int32)[None, :, None]
    return ((1 - side) * half + offset).astype(jnp.int32)


def draw_anchor_live(key, part):
    devices = PAIRS // PAIRS_DEV
    jitter = jax.random.randint(jax.random.fold_in(key, 31), (EVENTS, 2, devices), 0, PAIRS_DEV // 8 + 1)
    place = (jnp.arange(EVENTS)[:, None, None] * 2 + jnp.arange(2)[None, :, None]) * devices + jnp.arange(devices)[None, None, :]
    final = max(EVENTS * 2 * devices - 1, 1)
    count = PAIRS_DEV // 3 + 2 * PAIRS_DEV // 3 * place // final - jitter
    count_rows = jnp.repeat(count, PAIRS_DEV, axis=2)
    position = jnp.arange(PAIRS) % PAIRS_DEV
    return (position[None, None, :] < count_rows).astype(jnp.int32)


def set_ends(entries, stream_key, low, high):
    longest = entries.shape.index(max(entries.shape))
    spots = []
    for shift in (0, 1):
        where = [jax.random.randint(jax.random.fold_in(stream_key, axis), (), 0, length) for axis, length in enumerate(entries.shape)]
        where[longest] = (where[longest] + shift) % entries.shape[longest]
        spots.append(tuple(where))
    return entries.at[spots[0]].set(low).at[spots[1]].set(high)


def level_of(key, dims, pieces, least, high):
    factor_of = 1.0
    for axis_at, blocks in pieces:
        heights = jax.random.uniform(jax.random.fold_in(jax.random.fold_in(key, 6), axis_at), (blocks,), jnp.float32, least / len(pieces), high / len(pieces))
        factor_of = factor_of * jnp.repeat(jnp.exp(heights), dims[axis_at] // blocks).reshape((-1,) + (1,) * (len(dims) - 1 - axis_at))
    return factor_of


def bell_draw(own_key, dims, deviation, reach, split=(), held_as=jnp.bfloat16):
    factor_of = level_of(own_key, dims, split, -0.22, 0.18) if split else 1.0
    entries = jax.random.normal(own_key, dims, jnp.float32) * deviation * factor_of
    return jnp.minimum(jnp.maximum(entries, -reach), reach).astype(held_as)


def setup_inputs(seed: int = 0) -> dict:
    seeds = jax.random.split(jax.random.key(seed), 10)
    return {
        "query": draw_query(jax.random.fold_in(seeds[9], 71), 0),
        "key": draw_key(jax.random.fold_in(seeds[9], 71), 0),
        "value": bell_draw(seeds[2], (EVENTS, 2, NPTS, D), 1.0, 6.0, ((0, 16), (1, 2), (2, 8))),
        "pattern": draw_pattern(jax.random.fold_in(seeds[9], 71), 0),
        "out_weight": bell_draw(seeds[4], (D, D), D ** -0.5, 0.25),
        "served": set_ends(jax.random.randint(seeds[5], (EVENTS, 2, REQS, CAP), 0, PTS_DEV), jax.random.fold_in(seeds[5], 1), 0, PTS_DEV - 1).astype(jnp.int32),
        "anchor_rows": set_ends(jax.random.randint(seeds[6], (EVENTS, 2, PAIRS), 0, PTS_DEV), jax.random.fold_in(seeds[6], 1), 0, PTS_DEV - 1).astype(jnp.int32),
        "positive_slot": draw_positive_slot(jax.random.fold_in(seeds[9], 71), 0),
        "anchor_live": draw_anchor_live(jax.random.fold_in(seeds[9], 71), 0),
    }


NEGATIVE = -1e+30
SHARPNESS_SCALE = 0.07

def attend_view(queries, keys, values, blocks):
    head_dim = D // HEADS
    scale = head_dim ** (-0.5)
    head_keys = keys.astype(jnp.float32).reshape(NPTS, HEADS, head_dim)
    head_values = values.astype(jnp.float32).reshape(NPTS, HEADS, head_dim)
    span = 4 * BLOCK
    key_block = jnp.arange(NPTS, dtype=jnp.int32) // BLOCK

    def one_block(index):
        query_rows = lax.dynamic_slice_in_dim(queries, index * span, span, 0).astype(jnp.float32).reshape(span, HEADS, head_dim)
        pattern_rows = lax.dynamic_slice_in_dim(blocks, index * 4, 4, 0)
        allowed = jnp.repeat(pattern_rows, BLOCK, axis=0)[:, key_block] > 0
        scores = jnp.einsum('qhd,khd->hqk', query_rows, head_keys, precision=lax.Precision.HIGHEST) * scale
        scores = jnp.where(allowed[None], scores, NEGATIVE)
        highest = lax.optimization_barrier(jnp.max(scores, axis=-1, keepdims=True))
        weights = jnp.where(allowed[None], jnp.exp(scores - highest), 0.0)
        totals = lax.optimization_barrier(jnp.sum(weights, axis=-1))
        rounded = lax.optimization_barrier(weights.astype(jnp.bfloat16)).astype(jnp.float32)
        mixed = jnp.einsum('hqk,khd->qhd', rounded, head_values, precision=lax.Precision.HIGHEST) / totals.T[:, :, None]
        return mixed.reshape(span, D).astype(jnp.bfloat16)
    return lax.map(one_block, jnp.arange(NPTS // span, dtype=jnp.int32)).reshape(NPTS, D)

def reference(query, key, value, pattern, out_weight, served, anchor_rows, positive_slot, anchor_live):
    anchor_weight = out_weight.astype(jnp.float32)

    def event_step(carry, inputs):
        grad_sum, loss_sum, live_sum = carry
        queries, keys, values, blocks, served_rows, own_rows, positive, live_mask = inputs
        mixed = jnp.stack([attend_view(queries[0], keys[0], values[0], blocks[0]), attend_view(queries[1], keys[1], values[1], blocks[1])])
        embedding_rows = jnp.einsum('kxs,sf->kxf', mixed.astype(jnp.float32), anchor_weight, precision=lax.Precision.HIGHEST)
        inverse = lax.rsqrt(lax.optimization_barrier(jnp.sum(embedding_rows * embedding_rows, axis=-1)) + 1e-06)
        unit = (embedding_rows * inverse[..., None]).astype(jnp.bfloat16)
        owner_rows = jnp.arange(N_SEQ, dtype=jnp.int32)[:, None, None] * PTS_DEV + served_rows.reshape(2, N_SEQ, 2 * N_SEQ, CAP)
        picked = jnp.stack([unit[0][owner_rows[0]], unit[1][owner_rows[1]]])
        contender_vectors = picked.transpose(2, 0, 1, 3, 4).reshape(2 * N_SEQ, CANDS, D).astype(jnp.float32)
        anchor_index = jnp.arange(PAIRS, dtype=jnp.int32) // PAIRS_DEV * PTS_DEV + own_rows
        query_vectors = jnp.stack([unit[0][anchor_index[0]], unit[1][anchor_index[1]]])
        query_vectors = query_vectors.reshape(2 * N_SEQ, PAIRS_DEV, D).astype(jnp.float32)
        pairwise_scores = jnp.einsum('ftg,fyg->fty', query_vectors, contender_vectors, precision=lax.Precision.HIGHEST) / SHARPNESS_SCALE
        exponentiated_scores = jnp.exp(pairwise_scores)
        partition_totals = lax.optimization_barrier(jnp.sum(exponentiated_scores, axis=-1))
        log_total = jnp.log(partition_totals)
        correct_column = (jnp.arange(CANDS, dtype=jnp.int32)[None, None, :] == positive.reshape(2 * N_SEQ, PAIRS_DEV)[..., None]).astype(jnp.float32)
        active_queries = live_mask.reshape(2 * N_SEQ, PAIRS_DEV).astype(jnp.float32)
        loss_sum = loss_sum + jnp.sum(active_queries * (log_total - lax.optimization_barrier(jnp.sum(pairwise_scores * correct_column, axis=-1))))
        live_sum = live_sum + jnp.sum(active_queries)
        score_derivatives = active_queries[..., None] * (exponentiated_scores / partition_totals[..., None] - correct_column) / SHARPNESS_SCALE
        anchor_grads = jnp.einsum('rak,rkd->rad', score_derivatives, contender_vectors, precision=lax.Precision.HIGHEST).reshape(2, PAIRS, D)
        candidate_grads = jnp.einsum('rak,rad->rkd', score_derivatives, query_vectors, precision=lax.Precision.HIGHEST)
        candidate_grads = candidate_grads.reshape(2 * N_SEQ, 2, N_SEQ, CAP, D).transpose(1, 2, 0, 3, 4)
        gathered = []
        for side in range(2):
            grads = jnp.zeros((NPTS, D), jnp.float32).at[owner_rows[side].reshape(-1)].add(candidate_grads[side].reshape(-1, D))
            grads = grads.at[anchor_index[side]].add(anchor_grads[side])
            gathered.append(grads)
        unit_grads = jnp.stack(gathered)
        inner = lax.optimization_barrier(jnp.sum(embedding_rows * unit_grads, axis=-1))
        embedding_gradients = (inverse[..., None] * (unit_grads - embedding_rows * (inverse * inverse * inner)[..., None])).astype(jnp.bfloat16)
        loss_term = jnp.einsum('guh,guy->hy', mixed.astype(jnp.float32), embedding_gradients.astype(jnp.float32), precision=lax.Precision.HIGHEST)
        return ((grad_sum + loss_term, loss_sum, live_sum), mixed)
    start = (jnp.zeros((D, D), jnp.float32), jnp.zeros((), jnp.float32), jnp.zeros((), jnp.float32))
    finals, mixed = lax.scan(event_step, start, (query, key, value, pattern, served, anchor_rows, positive_slot, anchor_live))
    grad_total, loss_total, live_total = finals
    return (mixed, grad_total, loss_total / live_total)
```

```python
import functools

import jax
import jax.numpy as jnp
from jax import lax
from jax.experimental import pallas as pl
from jax.experimental.pallas import tpu as pltpu
from jax.sharding import PartitionSpec as P

HEADS = 16
BLOCK = 128
SHARPNESS_SCALE = 0.07
GROUP = 4
EXTRA = 16
LIST = 32
NEGATIVE = -1e30
LOG2E = 1.4426950408889634

F32 = jnp.float32
BF16 = jnp.bfloat16


def dot(a, b):
    return lax.dot_general(a, b, (((1,), (0,)), ((), ())), preferred_element_type=F32)


def dot_nt(a, b):
    return lax.dot_general(a, b, (((1,), (1,)), ((), ())), preferred_element_type=F32)


def flip(x):
    return jnp.transpose(x, (1, 0))


def pack_kernel(peers, rows, q_ref, k_ref, v_ref, pattern_ref, out_ref):
    width = q_ref.shape[1] // peers
    for at, ref in enumerate((q_ref, k_ref, v_ref)):
        turned = flip(ref[...])
        for j in range(peers):
            out_ref[j, at * width : (at + 1) * width, :] = turned[j * width : (j + 1) * width, :]
    blocks = pattern_ref.shape[1]
    allowed = (pattern_ref[...] > 0).astype(F32)
    before = lax.broadcasted_iota(jnp.int32, (blocks, blocks), 0)
    after = lax.broadcasted_iota(jnp.int32, (blocks, blocks), 1)
    rank = dot(allowed.astype(BF16), (before <= after).astype(BF16)) - 1.0
    place = lax.broadcasted_iota(jnp.int32, (LIST, blocks), 0).astype(F32)
    number = lax.broadcasted_iota(jnp.int32, (LIST, blocks), 1).astype(F32)
    lane = lax.broadcasted_iota(jnp.int32, (LIST, 128), 1)
    table = jnp.zeros((LIST, 128), F32)
    for r in range(rows):
        on = allowed[r : r + 1, :]
        count = jnp.sum(on, axis=1, keepdims=True)
        here = jnp.where(place < count, place, 0.0)
        hit = jnp.where(rank[r : r + 1, :] == here, on, 0.0)
        column = jnp.sum(hit * number, axis=1, keepdims=True)
        column = jnp.where(place[:, :1] == float(blocks), count, column)
        table = jnp.where(lane == r, column, table)
    lists = flip(table)[:EXTRA, :].astype(BF16)
    tail = jnp.concatenate(
        [lists, jnp.zeros((EXTRA, 128 - LIST), BF16)]
        + [jnp.zeros((EXTRA, 128), BF16)] * (q_ref.shape[0] // 128 - 1),
        axis=1,
    )
    for j in range(peers):
        out_ref[j, 3 * width : 3 * width + EXTRA, :] = tail


def pack(queries, keys, values, pattern, peers):
    points, width = queries.shape
    rows = 3 * (width // peers) + EXTRA
    return pl.pallas_call(
        functools.partial(pack_kernel, peers, pattern.shape[0]),
        out_shape=jax.ShapeDtypeStruct((peers, rows, points), BF16),
        in_specs=[pl.BlockSpec(memory_space=pltpu.VMEM)] * 4,
        out_specs=pl.BlockSpec(memory_space=pltpu.VMEM),
        compiler_params=pltpu.CompilerParams(vmem_limit_bytes=32 << 20),
        name="pack_heads",
    )(queries, keys, values, pattern)


def attend_kernel(
    peers, per_peer, table_ref, got_ref, out_ref, qb, kb, vb, item_row, item_step, s_buf, p_buf,
    peak_buf, fade_buf, accum
):
    blocks = peers * per_peer
    head = 32
    factor = head ** (-0.5) * LOG2E
    zero = jnp.zeros((head, BLOCK), BF16)
    ones = (lax.broadcasted_iota(jnp.int32, (EXTRA, BLOCK), 0) == 0).astype(F32).astype(BF16)

    @pl.loop(0, peers)
    def _(j):
        for b in range(per_peer):
            block = j * per_peer + b
            span = slice(b * BLOCK, (b + 1) * BLOCK)
            scaled = got_ref[j, 0 : 2 * head, span].astype(F32) * factor
            high = scaled.astype(BF16)
            low = (scaled - high.astype(F32)).astype(BF16)
            left = jnp.concatenate([high[:head], zero, low[:head], zero], axis=0)
            right = jnp.concatenate([zero, high[head:], zero, low[head:]], axis=0)
            qb[block, :, 0:BLOCK] = left
            qb[block, :, BLOCK : 2 * BLOCK] = right
            turned = got_ref[j, 2 * head : 4 * head, span]
            kb[block, :, :] = flip(jnp.concatenate([turned, turned], axis=0))
            vb[block, 0 : 2 * head, :] = got_ref[j, 4 * head : 6 * head, span]
            vb[block, 2 * head : 2 * head + EXTRA, :] = ones

    vb[blocks, :, :] = jnp.zeros((2 * head + EXTRA, BLOCK), BF16)
    s_buf[...] = jnp.zeros_like(s_buf)
    p_buf[...] = jnp.zeros_like(p_buf)
    peak_buf[...] = jnp.zeros_like(peak_buf)
    fade_buf[...] = jnp.zeros_like(fade_buf)
    accum[...] = jnp.zeros_like(accum)

    def list_row(i, items):
        steps = (table_ref[i, blocks] + GROUP - 1) // GROUP

        def list_step(t, items):
            item_row[items] = i
            item_step[items] = t
            return items + 1

        return lax.fori_loop(0, steps, list_step, items)

    items = lax.fori_loop(0, blocks, list_row, 0)

    def stage(t, best):
        now = lax.rem(t, 2)
        item = jnp.minimum(t, items - 1)
        row, first = item_row[item], item_step[item] * GROUP
        picked = [kb[table_ref[row, first + g]] for g in range(GROUP)]
        scores = dot(jnp.concatenate(picked, axis=0), qb[row])
        peak = jnp.max(scores.reshape(GROUP * BLOCK // 8, 8, 2 * BLOCK), axis=0)
        old_peak = peak_buf[1 - now, 0:1, :]
        item = jnp.clip(t - 1, 0, items - 1)
        best = jnp.where(item_step[item] == 0, NEGATIVE, best)
        new_best = jnp.maximum(best, old_peak)
        weights = jnp.exp2(s_buf[1 - now] - new_best).astype(BF16)
        fade = jnp.exp2(best - new_best)
        item = jnp.clip(t - 2, 0, items - 1)
        row, first = item_row[item], item_step[item] * GROUP
        picked = []
        for g in range(GROUP):
            real = first + g < table_ref[row, blocks]
            picked.append(vb[jnp.where(real, table_ref[row, first + g], blocks)])
        added = dot(jnp.concatenate(picked, axis=1), p_buf[now])
        total = accum[...] * fade_buf[now, 0:1, :] + added
        accum[...] = total
        share = pl.reciprocal(total[2 * head : 2 * head + 1, :])
        j, b = row // per_peer, lax.rem(row, per_peer)
        span = pl.ds(pl.multiple_of(b * BLOCK, BLOCK), BLOCK)
        out_ref[j, 0:head, span] = (total[0:head, 0:BLOCK] * share[:, 0:BLOCK]).astype(BF16)
        out_ref[j, head : 2 * head, span] = (
            total[head : 2 * head, BLOCK : 2 * BLOCK] * share[:, BLOCK : 2 * BLOCK]
        ).astype(BF16)
        p_buf[1 - now] = weights
        fade_buf[1 - now] = jnp.broadcast_to(fade, (8, 2 * BLOCK))
        s_buf[now] = scores
        peak_buf[now] = jnp.broadcast_to(jnp.max(peak, axis=0, keepdims=True), (8, 2 * BLOCK))
        return new_best

    lax.fori_loop(0, items + 2, stage, jnp.full((1, 2 * BLOCK), NEGATIVE, F32))


def attend(table, got, peers):
    points = got.shape[2]
    per_peer = points // BLOCK
    blocks = peers * per_peer
    most = blocks * (-(-blocks // GROUP))
    return pl.pallas_call(
        functools.partial(attend_kernel, peers, per_peer),
        out_shape=jax.ShapeDtypeStruct((peers, 64, points), BF16),
        in_specs=[
            pl.BlockSpec(memory_space=pltpu.SMEM),
            pl.BlockSpec(memory_space=pltpu.VMEM),
        ],
        out_specs=pl.BlockSpec(memory_space=pltpu.VMEM),
        scratch_shapes=[
            pltpu.VMEM((blocks, 128, 2 * BLOCK), BF16),
            pltpu.VMEM((blocks, BLOCK, 128), BF16),
            pltpu.VMEM((blocks + 1, 64 + EXTRA, BLOCK), BF16),
            pltpu.SMEM((most,), jnp.int32),
            pltpu.SMEM((most,), jnp.int32),
            pltpu.VMEM((2, GROUP * BLOCK, 2 * BLOCK), F32),
            pltpu.VMEM((2, GROUP * BLOCK, 2 * BLOCK), BF16),
            pltpu.VMEM((2, 8, 2 * BLOCK), F32),
            pltpu.VMEM((2, 8, 2 * BLOCK), F32),
            pltpu.VMEM((64 + EXTRA, 2 * BLOCK), F32),
        ],
        compiler_params=pltpu.CompilerParams(vmem_limit_bytes=40 << 20),
        name="attend",
    )(table, got)


def hand_out_kernel(turned_ref, served_ref, own_ref, mixed_ref, sent_ref, anchor_ref):
    turned = turned_ref[...]
    points = turned.shape[1]
    mixed_ref[...] = flip(turned)
    requests = served_ref.shape[0]

    def picks(rows):
        at = lax.broadcasted_iota(jnp.int32, (points, rows.shape[1]), 0)
        return (at == rows).astype(F32).astype(BF16)

    for r in range(0, requests, 2):
        both = jnp.concatenate([served_ref[r : r + 1, :], served_ref[r + 1 : r + 2, :]], axis=1)
        found = dot(turned, picks(both)).astype(BF16)
        sent_ref[r] = found[:, :BLOCK]
        sent_ref[r + 1] = found[:, BLOCK:]
    anchor_ref[...] = dot(turned, picks(own_ref[...])).astype(BF16)


def hand_out(turned, served, own_rows):
    width, points = turned.shape
    requests, capacity = served.shape
    anchors = own_rows.shape[1]
    return pl.pallas_call(
        hand_out_kernel,
        out_shape=(
            jax.ShapeDtypeStruct((points, width), BF16),
            jax.ShapeDtypeStruct((requests, width, capacity), BF16),
            jax.ShapeDtypeStruct((width, anchors), BF16),
        ),
        in_specs=[pl.BlockSpec(memory_space=pltpu.VMEM)] * 3,
        out_specs=[pl.BlockSpec(memory_space=pltpu.VMEM)] * 3,
        compiler_params=pltpu.CompilerParams(vmem_limit_bytes=40 << 20),
        name="hand_out",
    )(turned, served, own_rows)


def contrast_kernel(
    cand_ref, anchor_ref, weight_ref, slot_ref, live_ref, grad_ref, sums_ref, embed, unit, inverse,
    logits, grads
):
    pieces, width, capacity = cand_ref.shape
    anchors = anchor_ref.shape[1]
    step = 2
    span = step * capacity
    turned_weight = flip(weight_ref[...])

    def normalise(rows):
        e = dot(turned_weight, rows)
        inv = lax.rsqrt(jnp.sum(e * e, axis=0, keepdims=True) + 1e-06)
        return e, inv, (e * inv).astype(BF16)

    def back(e, inv, g):
        inner = jnp.sum(e * g, axis=0, keepdims=True)
        return (inv * (g - e * (inv * inv * inner))).astype(BF16)

    def rows_of(i):
        return jnp.concatenate([cand_ref[step * i + n] for n in range(step)], axis=1)

    own = anchor_ref[...]
    own_embed, own_inverse, own_unit = normalise(own)
    own_rows = flip(own_unit)

    def column(row):
        return flip(jnp.broadcast_to(row.astype(F32), (128, anchors)))[:, :1]

    slot = column(slot_ref[...])
    live = column(live_ref[...])
    position = lax.broadcasted_iota(jnp.int32, (anchors, span), 1).astype(F32)

    def forward(i, carry):
        total, right = carry
        e, inv, u = normalise(rows_of(i))
        embed[i] = e
        unit[i] = u
        inverse[i] = jnp.broadcast_to(inv, (8, span))
        score = dot(own_rows, u) / SHARPNESS_SCALE
        logits[i] = score
        hit = position == slot - (i * span).astype(F32)
        right = right + jnp.where(hit, score, 0.0)
        return total + jnp.exp(score), right

    nothing = jnp.zeros((anchors, span), F32)
    total, right = lax.fori_loop(0, pieces // step, forward, (nothing, nothing))
    total = jnp.sum(total, axis=1, keepdims=True)
    log_total = jnp.log(total)
    right = jnp.sum(right, axis=1, keepdims=True)
    loss = jnp.sum(live * (log_total - right), axis=0, keepdims=True)
    count = jnp.sum(live, axis=0, keepdims=True)
    row = lax.broadcasted_iota(jnp.int32, (8, 128), 0)
    sums_ref[...] = jnp.where(row == 0, loss, jnp.where(row == 1, count, 0.0))
    share = live / (total * SHARPNESS_SCALE)
    push = live / SHARPNESS_SCALE

    grad_ref[...] = jnp.zeros_like(grad_ref)
    grads[...] = jnp.zeros_like(grads)

    def backward(i, carry):
        hit = position == slot - (i * span).astype(F32)
        d = jnp.exp(logits[i]) * share - jnp.where(hit, push, 0.0)
        d = d.astype(BF16)
        grads[...] += dot_nt(unit[i], d)
        z = back(embed[i], inverse[i, 0:1, :], dot(own_unit, d))
        grad_ref[...] += dot_nt(rows_of(i), z)
        return carry

    lax.fori_loop(0, pieces // step, backward, 0)
    grad_ref[...] += dot_nt(own, back(own_embed, own_inverse, grads[...]))


def contrast(candidates, anchors, weight, slot, live):
    pieces, width, capacity = candidates.shape
    count = anchors.shape[1]
    steps, span = pieces // 2, 2 * capacity
    return pl.pallas_call(
        contrast_kernel,
        out_shape=(
            jax.ShapeDtypeStruct((width, width), F32),
            jax.ShapeDtypeStruct((8, 128), F32),
        ),
        in_specs=[pl.BlockSpec(memory_space=pltpu.VMEM)] * 5,
        out_specs=[pl.BlockSpec(memory_space=pltpu.VMEM)] * 2,
        scratch_shapes=[
            pltpu.VMEM((steps, width, span), F32),
            pltpu.VMEM((steps, width, span), BF16),
            pltpu.VMEM((steps, 8, span), F32),
            pltpu.VMEM((steps, count, span), F32),
            pltpu.VMEM((width, count), F32),
        ],
        compiler_params=pltpu.CompilerParams(vmem_limit_bytes=48 << 20),
        name="contrast",
    )(candidates, anchors, weight, slot, live)


def total_over_devices(grad, sums):
    near, far = ("view", "seq"), "event"
    close, away = lax.axis_size(near), lax.axis_size(far)
    shape = grad.shape
    share = grad.size // close // 128

    def pair(x):
        high = x.astype(BF16)
        low = (x - high.astype(F32)).astype(BF16)
        return jnp.concatenate([high, low], axis=0)

    def split_sum(got):
        summed = jnp.sum(got.astype(F32), axis=0)
        return summed[:share], summed[share : share + 8] + summed[share + 8 :]

    cut = grad.reshape(close, share, 128).astype(BF16)
    both = jnp.concatenate([cut, jnp.broadcast_to(pair(sums)[None], (close, 16, 128))], axis=1)
    part, sums = split_sum(lax.all_to_all(both, near, 0, 0, tiled=True))
    both = jnp.concatenate([part.astype(BF16), pair(sums)], axis=0)
    both = jnp.broadcast_to(both[None], (away,) + both.shape)
    part, sums = split_sum(lax.all_to_all(both, far, 0, 0, tiled=True))
    whole = jnp.broadcast_to(part.astype(BF16)[None], (close, share, 128))
    whole = lax.all_to_all(whole, near, 0, 0, tiled=True)
    return whole.astype(F32).reshape(shape), sums[0, 0] / sums[1, 0]


def per_device(
    query, key, value, pattern, out_weight, served, anchor_rows, positive_slot, anchor_live
):
    points, width = query.shape[2:]
    peers = lax.axis_size("seq")
    rows = pattern.shape[2]
    sent = pack(query[0, 0], key[0, 0], value[0, 0], pattern[0, 0], peers)
    got = lax.all_to_all(sent, "seq", 0, 0, tiled=True)
    part = 3 * (width // peers)
    table = got[:, part : part + rows, :LIST].astype(jnp.int32).reshape(peers * rows, LIST)
    turned = attend(table, got, peers)
    turned = lax.all_to_all(turned, "seq", 0, 0, tiled=True).reshape(width, points)
    mixed, outgoing, anchors = hand_out(turned, served[0, 0], anchor_rows[0])
    incoming = lax.all_to_all(outgoing, ("view", "seq"), 0, 0, tiled=True)
    grad, sums = contrast(incoming, anchors, out_weight, positive_slot[0], anchor_live[0])
    grad_total, loss = total_over_devices(grad, sums)
    return (mixed[None, None], grad_total, loss)


def solution(mesh):
    placed = (
        P("event", "view", "seq", None),
        P("event", "view", "seq", None),
        P("event", "view", "seq", None),
        P("event", "view", "seq", None),
        P(),
        P("event", "view", "seq", None),
        P("event", "view", "seq"),
        P("event", "view", "seq"),
        P("event", "view", "seq"),
    )
    return jax.shard_map(
        per_device,
        mesh=mesh,
        in_specs=placed,
        out_specs=(P("event", "view", "seq", None), P(), P()),
        check_vma=False,
    )
```

```python
import functools

import jax
import jax.numpy as jnp
from jax import lax
from jax.experimental import pallas as pl
from jax.experimental.pallas import tpu as pltpu
from jax.sharding import PartitionSpec as P

HEADS = 16
BLOCK = 128
SHARPNESS_SCALE = 0.07
GROUP = 2
ITEMS = 6
EXTRA = 16
EVENT_RUN = 8
LIST = 32
NEGATIVE = -1e30
LOG2E = 1.4426950408889634

F32 = jnp.float32
BF16 = jnp.bfloat16


def dot(a, b):
    return lax.dot_general(a, b, (((1,), (0,)), ((), ())), preferred_element_type=F32)


def dot_nt(a, b):
    return lax.dot_general(a, b, (((1,), (1,)), ((), ())), preferred_element_type=F32)


def flip(x):
    return jnp.transpose(x, (1, 0))


def pack_kernel(
    peers, rows, q_hbm, k_hbm, v_hbm, pattern_hbm, out_ref, q_ref, k_ref, v_ref, pattern_ref, sems
):
    points, full = q_ref.shape
    width = full // peers
    spans = [slice(at, at + BLOCK) for at in range(0, points, BLOCK)]
    copies = [pltpu.make_async_copy(pattern_hbm, pattern_ref, sems.at[0])]
    for n, (source, target) in enumerate(((v_hbm, v_ref), (q_hbm, q_ref), (k_hbm, k_ref))):
        for m, span in enumerate(spans):
            copies.append(
                pltpu.make_async_copy(
                    source.at[span, :], target.at[span, :], sems.at[1 + n * len(spans) + m]
                )
            )
    for copy in copies:
        copy.start()

    copies[0].wait()
    blocks = pattern_ref.shape[1]
    allowed = (pattern_ref[...] > 0).astype(F32)
    before = lax.broadcasted_iota(jnp.int32, (blocks, blocks), 0)
    after = lax.broadcasted_iota(jnp.int32, (blocks, blocks), 1)
    rank = dot(allowed.astype(BF16), (before <= after).astype(BF16)) - 1.0
    place = lax.broadcasted_iota(jnp.int32, (LIST, blocks), 0).astype(F32)
    number = lax.broadcasted_iota(jnp.int32, (LIST, blocks), 1).astype(F32)
    lane = lax.broadcasted_iota(jnp.int32, (LIST, 128), 1)
    table = jnp.zeros((LIST, 128), F32)
    for r in range(rows):
        on = allowed[r : r + 1, :]
        count = jnp.sum(on, axis=1, keepdims=True)
        here = jnp.where(place < count, place, 0.0)
        hit = jnp.where(rank[r : r + 1, :] == here, on, 0.0)
        column = jnp.sum(hit * number, axis=1, keepdims=True)
        column = jnp.where(place[:, :1] == float(blocks), count, column)
        table = jnp.where(lane == r, column, table)
    lists = flip(table)[:EXTRA, :].astype(BF16)
    tail = jnp.concatenate(
        [lists, jnp.zeros((EXTRA, 128 - LIST), BF16)]
        + [jnp.zeros((EXTRA, 128), BF16)] * (points // 128 - 1),
        axis=1,
    )
    for j in range(peers):
        out_ref[j, 3 * width : 3 * width + EXTRA, :] = tail

    for n, (at, ref) in enumerate(((2, v_ref), (0, q_ref))):
        for m, span in enumerate(spans):
            copies[1 + n * len(spans) + m].wait()
            turned = flip(ref[span, :])
            for j in range(peers):
                out_ref[j, at * width : (at + 1) * width, span] = turned[
                    j * width : (j + 1) * width, :
                ]
    for m, span in enumerate(spans):
        copies[1 + 2 * len(spans) + m].wait()
        for j in range(peers):
            cols = slice(j * width, (j + 1) * width)
            first = k_ref[span.start : span.start + width, cols]
            second = k_ref[span.start + width : span.stop, cols]
            out_ref[j, width : 2 * width, span] = jnp.concatenate([first, second], axis=1)


def pack(queries, keys, values, pattern, peers):
    points, width = queries.shape
    rows = 3 * (width // peers) + EXTRA
    return pl.pallas_call(
        functools.partial(pack_kernel, peers, pattern.shape[0]),
        out_shape=jax.ShapeDtypeStruct((peers, rows, points), BF16),
        in_specs=[pl.BlockSpec(memory_space=pl.ANY)] * 4,
        out_specs=pl.BlockSpec(memory_space=pltpu.VMEM),
        scratch_shapes=[
            pltpu.VMEM((points, width), BF16),
            pltpu.VMEM((points, width), BF16),
            pltpu.VMEM((points, width), BF16),
            pltpu.VMEM(pattern.shape, jnp.int32),
            pltpu.SemaphoreType.DMA((1 + 3 * (points // BLOCK),)),
        ],
        compiler_params=pltpu.CompilerParams(vmem_limit_bytes=60 << 20),
        name="pack_heads",
    )(queries, keys, values, pattern)


def four_rows(first, second):
    row = lax.broadcasted_iota(jnp.int32, (8, 128), 0)
    value = jnp.where(lax.rem(row, 2) == 0, first, second)
    high = value.astype(BF16).astype(F32)
    return jnp.where(row < 2, high, jnp.where(row < 4, value - high, 0.0)).astype(BF16)


def attend_kernel(
    peers, per_peer, table_ref, got_ref, out_ref, qb, kb, vb, scored, weighed, peak, fade, accum
):
    blocks = peers * per_peer
    head = 32
    factor = head ** (-0.5) * LOG2E
    zero = jnp.zeros((head, BLOCK), BF16)
    ones = (lax.broadcasted_iota(jnp.int32, (EXTRA, BLOCK), 0) == 0).astype(F32).astype(BF16)

    for j in range(peers):
        for b in range(per_peer):
            block = j * per_peer + b
            span = slice(b * BLOCK, (b + 1) * BLOCK)
            scaled = got_ref[j, 0 : 2 * head, span].astype(F32) * factor
            high = scaled.astype(BF16)
            low = (scaled - high.astype(F32)).astype(BF16)
            left = jnp.concatenate([high[:head], zero, low[:head], zero], axis=0)
            right = jnp.concatenate([zero, high[head:], zero, low[head:]], axis=0)
            qb[block, :, 0:BLOCK] = left
            qb[block, :, BLOCK : 2 * BLOCK] = right
            pair = got_ref[j, 2 * head : 4 * head, span]
            first, second = pair[:, : 2 * head], pair[:, 2 * head :]
            kb[block, : BLOCK // 2, :] = jnp.concatenate([first, first], axis=1)
            kb[block, BLOCK // 2 :, :] = jnp.concatenate([second, second], axis=1)
            vb[block, 0 : 2 * head, :] = got_ref[j, 4 * head : 6 * head, span]
            vb[block, 2 * head : 2 * head + EXTRA, :] = ones

    vb[blocks, :, :] = jnp.zeros((2 * head + EXTRA, BLOCK), BF16)
    for ref in (scored, weighed, peak, fade, accum):
        ref[...] = jnp.zeros_like(ref)

    steps_of = [(table_ref[i, blocks] + GROUP - 1) // GROUP for i in range(blocks)]
    items = functools.reduce(lambda x, y: x + y, steps_of)

    def after(item):
        row, step, real = item
        last = (step + 1) * GROUP >= table_ref[row, blocks]
        end = jnp.logical_and(last, row == blocks - 1)
        return (
            jnp.where(jnp.logical_and(last, row < blocks - 1), row + 1, row),
            jnp.where(end, step, jnp.where(last, 0, step + 1)),
            jnp.where(end, 0, real),
        )

    def turn(t, carry):
        best, at_scores, at_weights, at_sums = carry
        total = accum[...]
        for n, (row, step, real) in enumerate(at_sums):
            first = step * GROUP
            count = jnp.where(real == 1, table_ref[row, blocks], 0)
            picked = []
            for g in range(GROUP):
                picked.append(vb[jnp.where(first + g < count, table_ref[row, first + g], blocks)])
            added = dot(jnp.concatenate(picked, axis=1), weighed[n])
            total = total * fade[n, 0:1, :] + added
            share = pl.reciprocal(total[2 * head : 2 * head + 1, :])
            j, b = row // per_peer, lax.rem(row, per_peer)
            span = pl.ds(pl.multiple_of(b * BLOCK, BLOCK), BLOCK)
            out_ref[j, 0:head, span] = (total[0:head, 0:BLOCK] * share[:, 0:BLOCK]).astype(BF16)
            out_ref[j, head : 2 * head, span] = (
                total[head : 2 * head, BLOCK : 2 * BLOCK] * share[:, BLOCK : 2 * BLOCK]
            ).astype(BF16)
        accum[...] = total
        for n, (row, step, real) in enumerate(at_weights):
            best = jnp.where(jnp.logical_and(step == 0, real == 1), NEGATIVE, best)
            new_best = jnp.maximum(best, peak[n, 0:1, :])
            weighed[n] = jnp.exp2(scored[n] - new_best).astype(BF16)
            fade[n] = jnp.broadcast_to(jnp.exp2(best - new_best), (8, 2 * BLOCK))
            best = new_best
        for n, (row, step, real) in enumerate(at_scores):
            picked = [kb[table_ref[row, step * GROUP + g]] for g in range(GROUP)]
            scores = dot(jnp.concatenate(picked, axis=0), qb[row])
            scored[n] = scores
            top = jnp.max(scores.reshape(GROUP * BLOCK // 8, 8, 2 * BLOCK), axis=0)
            peak[n] = jnp.broadcast_to(jnp.max(top, axis=0, keepdims=True), (8, 2 * BLOCK))
        following = [after(at_scores[-1])]
        for n in range(ITEMS - 1):
            following.append(after(following[-1]))
        return best, tuple(following), at_scores, at_weights

    zero = jnp.int32(0)
    items_at = [(zero, zero, jnp.int32(1))]
    for n in range(ITEMS - 1):
        items_at.append(after(items_at[-1]))
    idle = ((zero, zero, zero),) * ITEMS
    lax.fori_loop(
        0,
        (items + ITEMS - 1) // ITEMS + 2,
        turn,
        (jnp.full((1, 2 * BLOCK), NEGATIVE, F32), tuple(items_at), idle, idle),
    )


def attend(table, got, peers):
    points = got.shape[2]
    per_peer = points // BLOCK
    blocks = peers * per_peer
    return pl.pallas_call(
        functools.partial(attend_kernel, peers, per_peer),
        out_shape=jax.ShapeDtypeStruct((peers, 64, points), BF16),
        in_specs=[
            pl.BlockSpec(memory_space=pltpu.SMEM),
            pl.BlockSpec(memory_space=pltpu.VMEM),
        ],
        out_specs=pl.BlockSpec(memory_space=pltpu.VMEM),
        scratch_shapes=[
            pltpu.VMEM((blocks, 128, 2 * BLOCK), BF16),
            pltpu.VMEM((blocks, BLOCK, 128), BF16),
            pltpu.VMEM((blocks + 1, 64 + EXTRA, BLOCK), BF16),
            pltpu.VMEM((ITEMS, GROUP * BLOCK, 2 * BLOCK), F32),
            pltpu.VMEM((ITEMS, GROUP * BLOCK, 2 * BLOCK), BF16),
            pltpu.VMEM((ITEMS, 8, 2 * BLOCK), F32),
            pltpu.VMEM((ITEMS, 8, 2 * BLOCK), F32),
            pltpu.VMEM((64 + EXTRA, 2 * BLOCK), F32),
        ],
        compiler_params=pltpu.CompilerParams(vmem_limit_bytes=40 << 20),
        name="attend",
    )(table, got)


def hand_out_kernel(turned_ref, served_ref, own_ref, mixed_ref, sent_ref, anchor_ref):
    turned = turned_ref[...]
    points = turned.shape[1]
    mixed_ref[...] = flip(turned)
    requests = served_ref.shape[0]

    def picks(rows):
        at = lax.broadcasted_iota(jnp.int32, (points, rows.shape[1]), 0)
        return (at == rows).astype(F32).astype(BF16)

    for r in range(0, requests, 2):
        both = jnp.concatenate([served_ref[r : r + 1, :], served_ref[r + 1 : r + 2, :]], axis=1)
        found = dot(turned, picks(both)).astype(BF16)
        sent_ref[r] = found[:, :BLOCK]
        sent_ref[r + 1] = found[:, BLOCK:]
    anchor_ref[...] = dot(turned, picks(own_ref[...])).astype(BF16)


def hand_out(turned, served, own_rows):
    width, points = turned.shape
    requests, capacity = served.shape
    anchors = own_rows.shape[1]
    return pl.pallas_call(
        hand_out_kernel,
        out_shape=(
            jax.ShapeDtypeStruct((points, width), BF16),
            jax.ShapeDtypeStruct((requests, width, capacity), BF16),
            jax.ShapeDtypeStruct((width, anchors), BF16),
        ),
        in_specs=[pl.BlockSpec(memory_space=pltpu.VMEM)] * 3,
        out_specs=[pl.BlockSpec(memory_space=pltpu.VMEM)] * 3,
        compiler_params=pltpu.CompilerParams(vmem_limit_bytes=40 << 20),
        name="hand_out",
    )(turned, served, own_rows)


def contrast_kernel(
    cand_ref, anchor_ref, weight_ref, slot_ref, live_ref, out_ref, embed, unit, inverse,
    expo, slopes, pulls
):
    pieces, width, capacity = cand_ref.shape
    anchors = anchor_ref.shape[1]
    span = 2 * capacity
    steps = pieces // 2
    turned_weight = flip(weight_ref[...])

    def normalise(rows):
        e = dot(turned_weight, rows)
        inv = lax.rsqrt(jnp.sum(e * e, axis=0, keepdims=True) + 1e-06)
        return e, inv, (e * inv).astype(BF16)

    def back(e, inv, g):
        inner = jnp.sum(e * g, axis=0, keepdims=True)
        return (inv * g - e * (inv * inv * inv * inner)).astype(BF16)

    def rows_of(i):
        return jnp.concatenate([cand_ref[2 * i], cand_ref[2 * i + 1]], axis=1)

    own = anchor_ref[...]
    own_embed, own_inverse, own_unit = normalise(own)
    own_rows = flip(own_unit)

    def column(row):
        return flip(jnp.broadcast_to(row.astype(F32), (128, anchors)))[:, :1]

    slot = column(slot_ref[...])
    live = column(live_ref[...])
    position = lax.broadcasted_iota(jnp.int32, (anchors, span), 1).astype(F32)
    sharpness = 1.0 / SHARPNESS_SCALE

    total = jnp.zeros((anchors, capacity), F32)
    right = jnp.zeros((anchors, capacity), F32)
    for i in range(steps):
        at = slice(i * span, (i + 1) * span)
        e, inv, u = normalise(rows_of(i))
        embed[:, at] = e
        unit[:, at] = u
        inverse[:, at] = jnp.broadcast_to(inv, (8, span))
        score = dot(own_rows, u)
        hit = position == slot - float(i * span)
        kept = jnp.where(hit, score, 0.0)
        right = right + (kept[:, :capacity] + kept[:, capacity:])
        grown = jnp.exp2(score * (sharpness * LOG2E))
        expo[:, at] = grown
        total = total + (grown[:, :capacity] + grown[:, capacity:])
    total = jnp.sum(total, axis=1, keepdims=True)
    right = jnp.sum(right, axis=1, keepdims=True) * sharpness
    loss = jnp.sum(live * (jnp.log(total) - right), axis=0, keepdims=True)
    count = jnp.sum(live, axis=0, keepdims=True)
    sums = four_rows(loss, count)
    share = live / total * sharpness
    push = live * sharpness

    for i in range(steps):
        at = slice(i * span, (i + 1) * span)
        hit = position == slot - float(i * span)
        d = (expo[:, at] * share - jnp.where(hit, push, 0.0)).astype(BF16)
        slopes[:, at] = d
        pulls[:, at] = back(embed[:, at], inverse[0:1, at], dot(own_unit, d))
    own_pull = back(own_embed, own_inverse, dot_nt(unit[...], slopes[...]))
    taken = jnp.concatenate([cand_ref[n] for n in range(pieces)], axis=1)
    ways = out_ref.shape[0]
    rows = width // ways
    half = width // 2
    for c in range(2):
        grad = dot_nt(taken, pulls[c * half : (c + 1) * half, :])
        grad = (grad + dot_nt(own, own_pull[c * half : (c + 1) * half, :])).astype(BF16)
        for j in range(ways):
            for m in range(half // 128):
                to = (c * (half // 128) + m) * rows
                out_ref[j, to : to + rows, :] = grad[
                    j * rows : (j + 1) * rows, m * 128 : (m + 1) * 128
                ]
    for j in range(ways):
        out_ref[j, rows * width // 128 :, :] = sums


def contrast(candidates, anchors, weight, slot, live, ways):
    pieces, width, capacity = candidates.shape
    count = anchors.shape[1]
    many = pieces * capacity
    return pl.pallas_call(
        contrast_kernel,
        out_shape=jax.ShapeDtypeStruct((ways, width * width // ways // 128 + 8, 128), BF16),
        in_specs=[pl.BlockSpec(memory_space=pltpu.VMEM)] * 5,
        out_specs=pl.BlockSpec(memory_space=pltpu.VMEM),
        scratch_shapes=[
            pltpu.VMEM((width, many), F32),
            pltpu.VMEM((width, many), BF16),
            pltpu.VMEM((8, many), F32),
            pltpu.VMEM((count, many), F32),
            pltpu.VMEM((count, many), BF16),
            pltpu.VMEM((width, many), BF16),
        ],
        compiler_params=pltpu.CompilerParams(vmem_limit_bytes=48 << 20),
        name="contrast",
    )(candidates, anchors, weight, slot, live)


def summed(got_ref):
    total = got_ref[0].astype(F32)
    for n in range(1, got_ref.shape[0]):
        total += got_ref[n].astype(F32)
    part, sums = total[:-8], total[-8:]
    return part, sums[0:1] + sums[2:3], sums[1:2] + sums[3:4]


def first_sum_kernel(got_ref, out_ref):
    part, loss, count = summed(got_ref)
    rows = part.shape[0]
    part = part.astype(BF16)
    sums = four_rows(loss, count)
    for n in range(out_ref.shape[0]):
        out_ref[n, :rows, :] = part
        out_ref[n, rows:, :] = sums


def last_sum_kernel(got_ref, out_ref, loss_ref):
    part, loss, count = summed(got_ref)
    rows = out_ref.shape[1]
    part = part.astype(BF16)
    whole = jnp.concatenate(
        [part[at : at + rows, :] for at in range(0, part.shape[0], rows)], axis=1
    )
    for n in range(out_ref.shape[0]):
        out_ref[n] = whole
    loss_ref[...] = loss / count


def groups():
    close = lax.axis_size(("view", "seq"))
    events = lax.axis_size("event")
    deep = EVENT_RUN if events % EVENT_RUN == 0 else events
    planes = [
        [near * events + far * deep + z for near in range(close) for far in range(events // deep)]
        for z in range(deep)
    ]
    lines = [[far * deep + z for z in range(deep)] for far in range(events // deep)]
    return planes, lines


def total_over_devices(parts, width):
    planes, lines = groups()
    everywhere = ("view", "seq", "event")
    vmem = pl.BlockSpec(memory_space=pltpu.VMEM)
    got = lax.all_to_all(parts, everywhere, 0, 0, axis_index_groups=planes, tiled=True)
    whole = pl.pallas_call(
        first_sum_kernel,
        out_shape=jax.ShapeDtypeStruct((len(lines[0]),) + parts.shape[1:], BF16),
        in_specs=[vmem],
        out_specs=vmem,
        name="first_sum",
    )(got)
    got = lax.all_to_all(whole, "event", 0, 0, axis_index_groups=lines, tiled=True)
    ways = len(planes[0])
    whole, loss = pl.pallas_call(
        last_sum_kernel,
        out_shape=(
            jax.ShapeDtypeStruct((ways, width // ways, width), BF16),
            jax.ShapeDtypeStruct((1, 128), F32),
        ),
        in_specs=[vmem],
        out_specs=[vmem, vmem],
        name="last_sum",
    )(got)
    grad = lax.all_to_all(whole, everywhere, 0, 0, axis_index_groups=planes, tiled=True)
    return grad.reshape(width, width).astype(F32), loss[0, 0]


def per_device(
    query, key, value, pattern, out_weight, served, anchor_rows, positive_slot, anchor_live
):
    points, width = query.shape[2:]
    peers = lax.axis_size("seq")
    rows = pattern.shape[2]
    sent = pack(query[0, 0], key[0, 0], value[0, 0], pattern[0, 0], peers)
    got = lax.all_to_all(sent, "seq", 0, 0, tiled=True)
    part = 3 * (width // peers)
    table = got[:, part : part + rows, :LIST].astype(jnp.int32).reshape(peers * rows, LIST)
    turned = attend(table, got, peers)
    turned = lax.all_to_all(turned, "seq", 0, 0, tiled=True).reshape(width, points)
    mixed, outgoing, anchors = hand_out(turned, served[0, 0], anchor_rows[0])
    incoming = lax.all_to_all(outgoing, ("view", "seq"), 0, 0, tiled=True)
    ways = len(groups()[0][0])
    parts = contrast(incoming, anchors, out_weight, positive_slot[0], anchor_live[0], ways)
    grad_total, loss = total_over_devices(parts, width)
    return (mixed[None, None], grad_total, loss)


def solution(mesh):
    placed = (
        P("event", "view", "seq", None),
        P("event", "view", "seq", None),
        P("event", "view", "seq", None),
        P("event", "view", "seq", None),
        P(),
        P("event", "view", "seq", None),
        P("event", "view", "seq"),
        P("event", "view", "seq"),
        P("event", "view", "seq"),
    )
    return jax.shard_map(
        per_device,
        mesh=mesh,
        in_specs=placed,
        out_specs=(P("event", "view", "seq", None), P(), P()),
        check_vma=False,
    )
```

```python
import functools

import jax
import jax.numpy as jnp
from jax import lax
from jax.experimental import pallas as pl
from jax.experimental.pallas import tpu as pltpu
from jax.sharding import PartitionSpec as P

HEADS = 16
BLOCK = 128
SHARPNESS_SCALE = 0.07
GROUP = 2
ITEMS = 6
EXTRA = 8
ONES = 16
EVENT_RUN = 8
LIST = 32
NEGATIVE = -1e30
LOG2E = 1.4426950408889634

F32 = jnp.float32
BF16 = jnp.bfloat16


def dot(a, b):
    return lax.dot_general(a, b, (((1,), (0,)), ((), ())), preferred_element_type=F32)


def dot_nt(a, b):
    return lax.dot_general(a, b, (((1,), (1,)), ((), ())), preferred_element_type=F32)


def flip(x):
    return jnp.transpose(x, (1, 0))


def pack_kernel(
    peers, rows, q_hbm, k_hbm, v_hbm, pattern_hbm, out_ref, q_ref, k_ref, v_ref, pattern_ref, sems
):
    points, full = q_ref.shape
    width = full // peers
    spans = [slice(at, at + BLOCK) for at in range(0, points, BLOCK)]
    copies = [pltpu.make_async_copy(pattern_hbm, pattern_ref, sems.at[0])]
    for n, (source, target) in enumerate(((v_hbm, v_ref), (q_hbm, q_ref), (k_hbm, k_ref))):
        for m, span in enumerate(spans):
            copies.append(
                pltpu.make_async_copy(
                    source.at[span, :], target.at[span, :], sems.at[1 + n * len(spans) + m]
                )
            )
    for copy in copies:
        copy.start()

    copies[0].wait()
    blocks = pattern_ref.shape[2]
    allowed = jnp.concatenate([pattern_ref[r] for r in range(rows)], axis=0)
    allowed = (allowed > 0).astype(F32)
    before = lax.broadcasted_iota(jnp.int32, (blocks, blocks), 0)
    after = lax.broadcasted_iota(jnp.int32, (blocks, blocks), 1)
    rank = dot(allowed.astype(BF16), (before <= after).astype(BF16)) - 1.0
    place = lax.broadcasted_iota(jnp.int32, (LIST, blocks), 0).astype(F32)
    number = lax.broadcasted_iota(jnp.int32, (LIST, blocks), 1).astype(F32)
    lane = lax.broadcasted_iota(jnp.int32, (LIST, 128), 1)
    table = jnp.zeros((LIST, 128), F32)
    for r in range(rows):
        on = allowed[r : r + 1, :]
        count = jnp.sum(on, axis=1, keepdims=True)
        here = jnp.where(place < count, place, 0.0)
        hit = jnp.where(rank[r : r + 1, :] == here, on, 0.0)
        column = jnp.sum(hit * number, axis=1, keepdims=True)
        column = jnp.where(place[:, :1] == float(blocks), count, column)
        table = jnp.where(lane == r, column, table)
    lists = flip(table)[:EXTRA, :].astype(BF16)
    tail = jnp.concatenate(
        [lists, jnp.zeros((EXTRA, 128 - LIST), BF16)]
        + [jnp.zeros((EXTRA, 128), BF16)] * (points // 128 - 1),
        axis=1,
    )
    for j in range(peers):
        out_ref[j, 3 * width : 3 * width + EXTRA, :] = tail

    for n, (at, ref) in enumerate(((2, v_ref), (0, q_ref))):
        for m, span in enumerate(spans):
            copies[1 + n * len(spans) + m].wait()
            turned = flip(ref[span, :])
            for j in range(peers):
                out_ref[j, at * width : (at + 1) * width, span] = turned[
                    j * width : (j + 1) * width, :
                ]
    for m, span in enumerate(spans):
        copies[1 + 2 * len(spans) + m].wait()
        for j in range(peers):
            cols = slice(j * width, (j + 1) * width)
            first = k_ref[span.start : span.start + width, cols]
            second = k_ref[span.start + width : span.stop, cols]
            out_ref[j, width : 2 * width, span] = jnp.concatenate([first, second], axis=1)


def pack(queries, keys, values, pattern, peers):
    points, width = queries.shape
    rows = 3 * (width // peers) + EXTRA
    return pl.pallas_call(
        functools.partial(pack_kernel, peers, pattern.shape[0]),
        out_shape=jax.ShapeDtypeStruct((peers, rows, points), BF16),
        in_specs=[pl.BlockSpec(memory_space=pl.ANY)] * 4,
        out_specs=pl.BlockSpec(memory_space=pltpu.VMEM),
        scratch_shapes=[
            pltpu.VMEM((points, width), BF16),
            pltpu.VMEM((points, width), BF16),
            pltpu.VMEM((points, width), BF16),
            pltpu.VMEM(pattern.shape, jnp.int32),
            pltpu.SemaphoreType.DMA((1 + 3 * (points // BLOCK),)),
        ],
        compiler_params=pltpu.CompilerParams(vmem_limit_bytes=60 << 20),
        name="pack_heads",
    )(queries, keys, values, pattern)


def four_rows(first, second):
    row = lax.broadcasted_iota(jnp.int32, (8, 128), 0)
    value = jnp.where(lax.rem(row, 2) == 0, first, second)
    high = value.astype(BF16).astype(F32)
    return jnp.where(row < 2, high, jnp.where(row < 4, value - high, 0.0)).astype(BF16)


def attend_kernel(
    peers, per_peer, table_ref, got_ref, out_ref, qb, kb, vb, scored, weighed, peak, fade, accum
):
    blocks = peers * per_peer
    head = 32
    factor = head ** (-0.5) * LOG2E
    zero = jnp.zeros((head, BLOCK), BF16)
    ones = (lax.broadcasted_iota(jnp.int32, (ONES, BLOCK), 0) == 0).astype(F32).astype(BF16)

    for j in range(peers):
        for b in range(per_peer):
            block = j * per_peer + b
            span = slice(b * BLOCK, (b + 1) * BLOCK)
            scaled = got_ref[j, 0 : 2 * head, span].astype(F32) * factor
            high = scaled.astype(BF16)
            low = (scaled - high.astype(F32)).astype(BF16)
            left = jnp.concatenate([high[:head], zero, low[:head], zero], axis=0)
            right = jnp.concatenate([zero, high[head:], zero, low[head:]], axis=0)
            qb[block, :, 0:BLOCK] = left
            qb[block, :, BLOCK : 2 * BLOCK] = right
            pair = got_ref[j, 2 * head : 4 * head, span]
            first, second = pair[:, : 2 * head], pair[:, 2 * head :]
            kb[block, : BLOCK // 2, :] = jnp.concatenate([first, first], axis=1)
            kb[block, BLOCK // 2 :, :] = jnp.concatenate([second, second], axis=1)
            vb[block, 0 : 2 * head, :] = got_ref[j, 4 * head : 6 * head, span]
            vb[block, 2 * head : 2 * head + ONES, :] = ones

    vb[blocks, :, :] = jnp.zeros((2 * head + ONES, BLOCK), BF16)
    for ref in (scored, weighed, peak, fade, accum):
        ref[...] = jnp.zeros_like(ref)

    steps_of = [(table_ref[i, blocks] + GROUP - 1) // GROUP for i in range(blocks)]
    items = functools.reduce(lambda x, y: x + y, steps_of)

    def after(item):
        row, step, real = item
        last = (step + 1) * GROUP >= table_ref[row, blocks]
        end = jnp.logical_and(last, row == blocks - 1)
        return (
            jnp.where(jnp.logical_and(last, row < blocks - 1), row + 1, row),
            jnp.where(end, step, jnp.where(last, 0, step + 1)),
            jnp.where(end, 0, real),
        )

    def turn(t, carry):
        best, at_scores, at_weights, at_sums = carry
        total = accum[...]
        for n, (row, step, real) in enumerate(at_sums):
            first = step * GROUP
            count = jnp.where(real == 1, table_ref[row, blocks], 0)
            picked = []
            for g in range(GROUP):
                picked.append(vb[jnp.where(first + g < count, table_ref[row, first + g], blocks)])
            added = dot(jnp.concatenate(picked, axis=1), weighed[n])
            total = total * fade[n, 0:1, :] + added
            share = pl.reciprocal(total[2 * head : 2 * head + 1, :])
            j, b = row // per_peer, lax.rem(row, per_peer)
            span = pl.ds(pl.multiple_of(b * BLOCK, BLOCK), BLOCK)
            out_ref[j, 0:head, span] = (total[0:head, 0:BLOCK] * share[:, 0:BLOCK]).astype(BF16)
            out_ref[j, head : 2 * head, span] = (
                total[head : 2 * head, BLOCK : 2 * BLOCK] * share[:, BLOCK : 2 * BLOCK]
            ).astype(BF16)
        accum[...] = total
        for n, (row, step, real) in enumerate(at_weights):
            best = jnp.where(jnp.logical_and(step == 0, real == 1), NEGATIVE, best)
            new_best = jnp.maximum(best, peak[n, 0:1, :])
            weighed[n] = jnp.exp2(scored[n] - new_best).astype(BF16)
            fade[n] = jnp.broadcast_to(jnp.exp2(best - new_best), (8, 2 * BLOCK))
            best = new_best
        for n, (row, step, real) in enumerate(at_scores):
            picked = [kb[table_ref[row, step * GROUP + g]] for g in range(GROUP)]
            scores = dot(jnp.concatenate(picked, axis=0), qb[row])
            scored[n] = scores
            top = jnp.max(scores.reshape(GROUP * BLOCK // 8, 8, 2 * BLOCK), axis=0)
            peak[n] = jnp.broadcast_to(jnp.max(top, axis=0, keepdims=True), (8, 2 * BLOCK))
        following = [after(at_scores[-1])]
        for n in range(ITEMS - 1):
            following.append(after(following[-1]))
        return best, tuple(following), at_scores, at_weights

    zero = jnp.int32(0)
    items_at = [(zero, zero, jnp.int32(1))]
    for n in range(ITEMS - 1):
        items_at.append(after(items_at[-1]))
    idle = ((zero, zero, zero),) * ITEMS
    lax.fori_loop(
        0,
        (items + ITEMS - 1) // ITEMS + 2,
        turn,
        (jnp.full((1, 2 * BLOCK), NEGATIVE, F32), tuple(items_at), idle, idle),
    )


def attend(table, got, peers):
    points = got.shape[2]
    per_peer = points // BLOCK
    blocks = peers * per_peer
    return pl.pallas_call(
        functools.partial(attend_kernel, peers, per_peer),
        out_shape=jax.ShapeDtypeStruct((peers, 64, points), BF16),
        in_specs=[
            pl.BlockSpec(memory_space=pltpu.SMEM),
            pl.BlockSpec(memory_space=pltpu.VMEM),
        ],
        out_specs=pl.BlockSpec(memory_space=pltpu.VMEM),
        scratch_shapes=[
            pltpu.VMEM((blocks, 128, 2 * BLOCK), BF16),
            pltpu.VMEM((blocks, BLOCK, 128), BF16),
            pltpu.VMEM((blocks + 1, 64 + ONES, BLOCK), BF16),
            pltpu.VMEM((ITEMS, GROUP * BLOCK, 2 * BLOCK), F32),
            pltpu.VMEM((ITEMS, GROUP * BLOCK, 2 * BLOCK), BF16),
            pltpu.VMEM((ITEMS, 8, 2 * BLOCK), F32),
            pltpu.VMEM((ITEMS, 8, 2 * BLOCK), F32),
            pltpu.VMEM((64 + ONES, 2 * BLOCK), F32),
        ],
        compiler_params=pltpu.CompilerParams(vmem_limit_bytes=40 << 20),
        name="attend",
    )(table, got)


def hand_out_kernel(turned_ref, served_ref, own_ref, mixed_ref, sent_ref, anchor_ref):
    turned = turned_ref[...]
    points = turned.shape[1]
    mixed_ref[...] = flip(turned)
    requests = served_ref.shape[0]

    def picks(rows):
        at = lax.broadcasted_iota(jnp.int32, (points, rows.shape[1]), 0)
        return (at == rows).astype(F32).astype(BF16)

    for r in range(0, requests, 2):
        both = jnp.concatenate([served_ref[r : r + 1, :], served_ref[r + 1 : r + 2, :]], axis=1)
        found = dot(turned, picks(both)).astype(BF16)
        sent_ref[r] = found[:, :BLOCK]
        sent_ref[r + 1] = found[:, BLOCK:]
    anchor_ref[...] = dot(turned, picks(own_ref[...])).astype(BF16)


def hand_out(turned, served, own_rows):
    width, points = turned.shape
    requests, capacity = served.shape
    anchors = own_rows.shape[1]
    return pl.pallas_call(
        hand_out_kernel,
        out_shape=(
            jax.ShapeDtypeStruct((points, width), BF16),
            jax.ShapeDtypeStruct((requests, width, capacity), BF16),
            jax.ShapeDtypeStruct((width, anchors), BF16),
        ),
        in_specs=[pl.BlockSpec(memory_space=pltpu.VMEM)] * 3,
        out_specs=[pl.BlockSpec(memory_space=pltpu.VMEM)] * 3,
        compiler_params=pltpu.CompilerParams(vmem_limit_bytes=40 << 20),
        name="hand_out",
    )(turned, served, own_rows)


def contrast_kernel(
    cand_ref, anchor_ref, weight_ref, slot_ref, live_ref, away_ref, kept_ref, embed, unit, inverse,
    expo, slopes, pulls, own_pulls
):
    pieces, width, capacity = cand_ref.shape
    anchors = anchor_ref.shape[1]
    span = 2 * capacity
    steps = pieces // 2
    turned_weight = flip(weight_ref[...])

    def normalise(rows):
        e = dot(turned_weight, rows)
        inv = lax.rsqrt(jnp.sum(e * e, axis=0, keepdims=True) + 1e-06)
        return e, inv, (e * inv).astype(BF16)

    def back(e, inv, g):
        inner = jnp.sum(e * g, axis=0, keepdims=True)
        return (inv * g - e * (inv * inv * inv * inner)).astype(BF16)

    def rows_of(i):
        return jnp.concatenate([cand_ref[2 * i], cand_ref[2 * i + 1]], axis=1)

    own = anchor_ref[...]
    own_embed, own_inverse, own_unit = normalise(own)
    own_rows = flip(own_unit)

    def column(row):
        return flip(jnp.broadcast_to(row.astype(F32), (128, anchors)))[:, :1]

    slot = column(slot_ref[...])
    live = column(live_ref[...])
    position = lax.broadcasted_iota(jnp.int32, (anchors, span), 1).astype(F32)
    sharpness = 1.0 / SHARPNESS_SCALE

    total = jnp.zeros((anchors, capacity), F32)
    right = jnp.zeros((anchors, capacity), F32)
    for i in range(steps):
        at = slice(i * span, (i + 1) * span)
        e, inv, u = normalise(rows_of(i))
        embed[:, at] = e
        unit[:, at] = u
        inverse[:, at] = jnp.broadcast_to(inv, (8, span))
        score = dot(own_rows, u)
        hit = position == slot - float(i * span)
        kept = jnp.where(hit, score, 0.0)
        right = right + (kept[:, :capacity] + kept[:, capacity:])
        grown = jnp.exp2(score * (sharpness * LOG2E))
        expo[:, at] = grown
        total = total + (grown[:, :capacity] + grown[:, capacity:])
    total = jnp.sum(total, axis=1, keepdims=True)
    right = jnp.sum(right, axis=1, keepdims=True) * sharpness
    loss = jnp.sum(live * (jnp.log(total) - right), axis=0, keepdims=True)
    count = jnp.sum(live, axis=0, keepdims=True)
    sums = four_rows(loss, count)
    share = live / total * sharpness
    push = live * sharpness

    for i in range(steps):
        at = slice(i * span, (i + 1) * span)
        hit = position == slot - float(i * span)
        d = (expo[:, at] * share - jnp.where(hit, push, 0.0)).astype(BF16)
        slopes[:, at] = d
        pulls[:, at] = back(embed[:, at], inverse[0:1, at], dot(own_unit, d))
    own_pulls[...] = back(own_embed, own_inverse, dot_nt(unit[...], slopes[...]))
    taken = jnp.concatenate([cand_ref[n] for n in range(pieces)], axis=1)
    ways = kept_ref.shape[0]
    rows = width // ways
    half = width // 2
    core = lax.rem(lax.axis_index("seq"), 2)
    for out_ref, mine in ((away_ref, 1 - core), (kept_ref, core)):
        at = pl.ds(pl.multiple_of(mine * half, half), half)
        grad = dot_nt(taken, pulls[at, :])
        grad = (grad + dot_nt(own, own_pulls[at, :])).astype(BF16)
        for j in range(ways):
            for m in range(half // 128):
                out_ref[j, m * rows : (m + 1) * rows, :] = grad[
                    j * rows : (j + 1) * rows, m * 128 : (m + 1) * 128
                ]
            out_ref[j, rows * half // 128 :, :] = sums


def contrast(candidates, anchors, weight, slot, live, ways):
    pieces, width, capacity = candidates.shape
    count = anchors.shape[1]
    many = pieces * capacity
    half = jax.ShapeDtypeStruct((ways, width * width // 2 // ways // 128 + 8, 128), BF16)
    return pl.pallas_call(
        contrast_kernel,
        out_shape=(half,) * 2,
        in_specs=[pl.BlockSpec(memory_space=pltpu.VMEM)] * 5,
        out_specs=[pl.BlockSpec(memory_space=pltpu.VMEM)] * 2,
        scratch_shapes=[
            pltpu.VMEM((width, many), F32),
            pltpu.VMEM((width, many), BF16),
            pltpu.VMEM((8, many), F32),
            pltpu.VMEM((count, many), F32),
            pltpu.VMEM((count, many), BF16),
            pltpu.VMEM((width, many), BF16),
            pltpu.VMEM((width, count), BF16),
        ],
        compiler_params=pltpu.CompilerParams(vmem_limit_bytes=48 << 20),
        name="contrast",
    )(candidates, anchors, weight, slot, live)


def summed(got_ref):
    total = got_ref[0].astype(F32)
    for n in range(1, got_ref.shape[0]):
        total += got_ref[n].astype(F32)
    part, sums = total[:-8], total[-8:]
    return part, sums[0:1] + sums[2:3], sums[1:2] + sums[3:4]


def first_sum_kernel(got_ref, out_ref):
    part, loss, count = summed(got_ref)
    rows = part.shape[0]
    part = part.astype(BF16)
    sums = four_rows(loss, count)
    for n in range(out_ref.shape[0]):
        out_ref[n, :rows, :] = part
        out_ref[n, rows:, :] = sums


def last_sum_kernel(got_ref, out_ref, loss_ref):
    part, loss, count = summed(got_ref)
    rows = out_ref.shape[1]
    part = part.astype(BF16)
    whole = jnp.concatenate(
        [part[at : at + rows, :] for at in range(0, part.shape[0], rows)], axis=1
    )
    for n in range(out_ref.shape[0]):
        out_ref[n] = whole
    loss_ref[...] = loss / count


def core_sum_kernel(one_ref, two_ref, out_ref):
    rows = out_ref.shape[1] - 8
    total = one_ref[:, :rows, :].astype(F32) + two_ref[:, :rows, :].astype(F32)
    sums = one_ref[0, rows:, :].astype(F32) + two_ref[0, rows:, :].astype(F32)
    sums = four_rows(sums[0:1] + sums[2:3], sums[1:2] + sums[3:4])
    out_ref[:, :rows, :] = total.astype(BF16)
    for n in range(out_ref.shape[0]):
        out_ref[n, rows:, :] = sums


def groups():
    close = lax.axis_size(("view", "seq"))
    events = lax.axis_size("event")
    deep = EVENT_RUN if events % EVENT_RUN == 0 else events
    planes = [
        [
            near * events + far * deep + z
            for near in range(core, close, 2)
            for far in range(events // deep)
        ]
        for core in range(2)
        for z in range(deep)
    ]
    lines = [[far * deep + z for z in range(deep)] for far in range(events // deep)]
    return planes, lines


def to_other_core(x):
    peers = lax.axis_size("seq")
    return lax.ppermute(x, "seq", [(i, i ^ 1) for i in range(peers)])


def small(kernel, name, out_shape, *operands):
    vmem = pl.BlockSpec(memory_space=pltpu.VMEM)
    return pl.pallas_call(
        kernel,
        out_shape=out_shape,
        in_specs=[vmem] * len(operands),
        out_specs=jax.tree.map(lambda shape: vmem, out_shape),
        compiler_params=pltpu.CompilerParams(vmem_limit_bytes=12 << 20),
        name=name,
    )(*operands)


def total_over_devices(away, kept, core, width):
    planes, lines = groups()
    everywhere = ("view", "seq", "event")
    ways, half = len(planes[0]), width // 2
    shape = kept.shape
    parts = small(
        core_sum_kernel, "core_sum", jax.ShapeDtypeStruct(shape, BF16), kept, to_other_core(away)
    )
    got = lax.all_to_all(parts, everywhere, 0, 0, axis_index_groups=planes, tiled=True)
    whole = small(
        first_sum_kernel, "first_sum", jax.ShapeDtypeStruct((len(lines[0]),) + shape[1:], BF16), got
    )
    got = lax.all_to_all(whole, "event", 0, 0, axis_index_groups=lines, tiled=True)
    whole, loss = small(
        last_sum_kernel,
        "last_sum",
        (
            jax.ShapeDtypeStruct((ways, width // ways, half), BF16),
            jax.ShapeDtypeStruct((1, 128), F32),
        ),
        got,
    )
    mine = lax.all_to_all(whole, everywhere, 0, 0, axis_index_groups=planes, tiled=True)
    mine = mine.reshape(width, half)
    other = to_other_core(mine)
    grad = jnp.where(
        core == 0,
        jnp.concatenate([mine, other], axis=1),
        jnp.concatenate([other, mine], axis=1),
    )
    return grad.astype(F32), loss[0, 0]


def per_device(
    query, key, value, pattern, out_weight, served, anchor_rows, positive_slot, anchor_live
):
    points, width = query.shape[2:]
    peers = lax.axis_size("seq")
    rows = pattern.shape[2]
    sent = pack(query[0, 0], key[0, 0], value[0, 0], pattern[0, 0][:, None, :], peers)
    sent, core = lax.optimization_barrier((sent, lax.rem(lax.axis_index("seq"), 2)))
    got = lax.all_to_all(sent, "seq", 0, 0, tiled=True)
    part = 3 * (width // peers)
    table = got[:, part : part + rows, :LIST].astype(jnp.int32).reshape(peers * rows, LIST)
    turned = attend(table, got, peers)
    turned = lax.all_to_all(turned, "seq", 0, 0, tiled=True).reshape(width, points)
    mixed, outgoing, anchors = hand_out(turned, served[0, 0], anchor_rows[0])
    incoming = lax.all_to_all(outgoing, ("view", "seq"), 0, 0, tiled=True)
    ways = len(groups()[0][0])
    away, kept = contrast(
        incoming, anchors, out_weight, positive_slot[0], anchor_live[0], ways
    )
    grad_total, loss = total_over_devices(away, kept, core, width)
    return (mixed[None, None], grad_total, loss)


def solution(mesh):
    placed = (
        P("event", "view", "seq", None),
        P("event", "view", "seq", None),
        P("event", "view", "seq", None),
        P("event", "view", "seq", None),
        P(),
        P("event", "view", "seq", None),
        P("event", "view", "seq"),
        P("event", "view", "seq"),
        P("event", "view", "seq"),
    )
    return jax.shard_map(
        per_device,
        mesh=mesh,
        in_specs=placed,
        out_specs=(P("event", "view", "seq", None), P(), P()),
        check_vma=False,
    )
```

```python
import functools

import jax
import jax.numpy as jnp
from jax import lax
from jax.experimental import pallas as pl
from jax.experimental.pallas import tpu as pltpu
from jax.sharding import PartitionSpec as P

HEADS = 16
BLOCK = 128
SHARPNESS_SCALE = 0.07
GROUP = 2
ITEMS = 6
EXTRA = 8
ONES = 16
EVENT_RUN = 8
LIST = 32
NEGATIVE = -1e30
LOG2E = 1.4426950408889634

F32 = jnp.float32
BF16 = jnp.bfloat16


def dot(a, b):
    return lax.dot_general(a, b, (((1,), (0,)), ((), ())), preferred_element_type=F32)


def dot_nt(a, b):
    return lax.dot_general(a, b, (((1,), (1,)), ((), ())), preferred_element_type=F32)


def flip(x):
    return jnp.transpose(x, (1, 0))


def pack_kernel(
    peers, rows, q_hbm, k_hbm, v_hbm, pattern_hbm, out_ref, q_ref, k_ref, v_ref, pattern_ref, sems
):
    points, full = q_ref.shape
    width = full // peers
    spans = [slice(at, at + BLOCK) for at in range(0, points, BLOCK)]
    copies = [pltpu.make_async_copy(pattern_hbm, pattern_ref, sems.at[0])]
    for n, (source, target) in enumerate(((v_hbm, v_ref), (q_hbm, q_ref), (k_hbm, k_ref))):
        for m, span in enumerate(spans):
            copies.append(
                pltpu.make_async_copy(
                    source.at[span, :], target.at[span, :], sems.at[1 + n * len(spans) + m]
                )
            )
    for copy in copies:
        copy.start()

    copies[0].wait()
    blocks = pattern_ref.shape[2]
    allowed = jnp.concatenate([pattern_ref[r] for r in range(rows)], axis=0)
    allowed = (allowed > 0).astype(F32)
    before = lax.broadcasted_iota(jnp.int32, (blocks, blocks), 0)
    after = lax.broadcasted_iota(jnp.int32, (blocks, blocks), 1)
    rank = dot(allowed.astype(BF16), (before <= after).astype(BF16)) - 1.0
    place = lax.broadcasted_iota(jnp.int32, (LIST, blocks), 0).astype(F32)
    number = lax.broadcasted_iota(jnp.int32, (LIST, blocks), 1).astype(F32)
    lane = lax.broadcasted_iota(jnp.int32, (LIST, 128), 1)
    table = jnp.zeros((LIST, 128), F32)
    for r in range(rows):
        on = allowed[r : r + 1, :]
        count = jnp.sum(on, axis=1, keepdims=True)
        here = jnp.where(place < count, place, 0.0)
        hit = jnp.where(rank[r : r + 1, :] == here, on, 0.0)
        column = jnp.sum(hit * number, axis=1, keepdims=True)
        column = jnp.where(place[:, :1] == float(blocks), count, column)
        table = jnp.where(lane == r, column, table)
    lists = flip(table)[:EXTRA, :].astype(BF16)
    tail = jnp.concatenate(
        [lists, jnp.zeros((EXTRA, 128 - LIST), BF16)]
        + [jnp.zeros((EXTRA, 128), BF16)] * (points // 128 - 1),
        axis=1,
    )
    for j in range(peers):
        out_ref[j, 3 * width : 3 * width + EXTRA, :] = tail

    for n, (at, ref) in enumerate(((2, v_ref), (0, q_ref))):
        for m, span in enumerate(spans):
            copies[1 + n * len(spans) + m].wait()
            turned = flip(ref[span, :])
            for j in range(peers):
                out_ref[j, at * width : (at + 1) * width, span] = turned[
                    j * width : (j + 1) * width, :
                ]
    for m, span in enumerate(spans):
        copies[1 + 2 * len(spans) + m].wait()
        for j in range(peers):
            cols = slice(j * width, (j + 1) * width)
            first = k_ref[span.start : span.start + width, cols]
            second = k_ref[span.start + width : span.stop, cols]
            out_ref[j, width : 2 * width, span] = jnp.concatenate([first, second], axis=1)


def pack(queries, keys, values, pattern, peers):
    points, width = queries.shape
    rows = 3 * (width // peers) + EXTRA
    return pl.pallas_call(
        functools.partial(pack_kernel, peers, pattern.shape[0]),
        out_shape=jax.ShapeDtypeStruct((peers, rows, points), BF16),
        in_specs=[pl.BlockSpec(memory_space=pltpu.HBM)] * 4,
        out_specs=pl.BlockSpec(memory_space=pltpu.VMEM),
        scratch_shapes=[
            pltpu.VMEM((points, width), BF16),
            pltpu.VMEM((points, width), BF16),
            pltpu.VMEM((points, width), BF16),
            pltpu.VMEM(pattern.shape, jnp.int32),
            pltpu.SemaphoreType.DMA((1 + 3 * (points // BLOCK),)),
        ],
        compiler_params=pltpu.CompilerParams(vmem_limit_bytes=16 << 20),
        name="pack_heads",
    )(*(pltpu.with_memory_space_constraint(x, pltpu.HBM) for x in (queries, keys, values, pattern)))


def four_rows(first, second):
    row = lax.broadcasted_iota(jnp.int32, (8, 128), 0)
    value = jnp.where(lax.rem(row, 2) == 0, first, second)
    high = value.astype(BF16).astype(F32)
    return jnp.where(row < 2, high, jnp.where(row < 4, value - high, 0.0)).astype(BF16)


def attend_kernel(
    peers, per_peer, table_ref, got_ref, out_ref, qb, kb, vb, scored, weighed, peak, fade, accum
):
    blocks = peers * per_peer
    head = 32
    factor = head ** (-0.5) * LOG2E
    zero = jnp.zeros((head, BLOCK), BF16)
    ones = (lax.broadcasted_iota(jnp.int32, (ONES, BLOCK), 0) == 0).astype(F32).astype(BF16)

    for j in range(peers):
        for b in range(per_peer):
            block = j * per_peer + b
            span = slice(b * BLOCK, (b + 1) * BLOCK)
            scaled = got_ref[j, 0 : 2 * head, span].astype(F32) * factor
            high = scaled.astype(BF16)
            low = (scaled - high.astype(F32)).astype(BF16)
            left = jnp.concatenate([high[:head], zero, low[:head], zero], axis=0)
            right = jnp.concatenate([zero, high[head:], zero, low[head:]], axis=0)
            qb[block, :, 0:BLOCK] = left
            qb[block, :, BLOCK : 2 * BLOCK] = right
            pair = got_ref[j, 2 * head : 4 * head, span]
            first, second = pair[:, : 2 * head], pair[:, 2 * head :]
            kb[block, : BLOCK // 2, :] = jnp.concatenate([first, first], axis=1)
            kb[block, BLOCK // 2 :, :] = jnp.concatenate([second, second], axis=1)
            vb[block, 0 : 2 * head, :] = got_ref[j, 4 * head : 6 * head, span]
            vb[block, 2 * head : 2 * head + ONES, :] = ones

    vb[blocks, :, :] = jnp.zeros((2 * head + ONES, BLOCK), BF16)
    steps_of = [(table_ref[i, blocks] + GROUP - 1) // GROUP for i in range(blocks)]
    items = functools.reduce(lambda x, y: x + y, steps_of)

    def after(item):
        row, step, real = item
        last = (step + 1) * GROUP >= table_ref[row, blocks]
        end = jnp.logical_and(last, row == blocks - 1)
        return (
            jnp.where(jnp.logical_and(last, row < blocks - 1), row + 1, row),
            jnp.where(end, step, jnp.where(last, 0, step + 1)),
            jnp.where(end, 0, real),
        )

    def turn(t, carry):
        best, at_scores, at_weights, at_sums = carry
        total = jnp.where(t < 3, 0.0, accum[...])
        for n, (row, step, real) in enumerate(at_sums):
            first = step * GROUP
            count = jnp.where(real == 1, table_ref[row, blocks], 0)
            picked = []
            for g in range(GROUP):
                picked.append(vb[jnp.where(first + g < count, table_ref[row, first + g], blocks)])
            added = dot(jnp.concatenate(picked, axis=1), weighed[n])
            total = total * fade[n, 0:1, :] + added
            share = pl.reciprocal(total[2 * head : 2 * head + 1, :])
            j, b = row // per_peer, lax.rem(row, per_peer)
            span = pl.ds(pl.multiple_of(b * BLOCK, BLOCK), BLOCK)
            out_ref[j, 0:head, span] = (total[0:head, 0:BLOCK] * share[:, 0:BLOCK]).astype(BF16)
            out_ref[j, head : 2 * head, span] = (
                total[head : 2 * head, BLOCK : 2 * BLOCK] * share[:, BLOCK : 2 * BLOCK]
            ).astype(BF16)
        accum[...] = total
        for n, (row, step, real) in enumerate(at_weights):
            best = jnp.where(jnp.logical_and(step == 0, real == 1), NEGATIVE, best)
            new_best = jnp.maximum(best, peak[n, 0:1, :])
            weighed[n] = jnp.exp2(scored[n] - new_best).astype(BF16)
            fade[n] = jnp.broadcast_to(jnp.exp2(best - new_best), (8, 2 * BLOCK))
            best = new_best
        for n, (row, step, real) in enumerate(at_scores):
            picked = [kb[table_ref[row, step * GROUP + g]] for g in range(GROUP)]
            scores = dot(jnp.concatenate(picked, axis=0), qb[row])
            scored[n] = scores
            top = jnp.max(scores.reshape(GROUP * BLOCK // 8, 8, 2 * BLOCK), axis=0)
            peak[n] = jnp.broadcast_to(jnp.max(top, axis=0, keepdims=True), (8, 2 * BLOCK))
        following = [after(at_scores[-1])]
        for n in range(ITEMS - 1):
            following.append(after(following[-1]))
        return best, tuple(following), at_scores, at_weights

    zero = jnp.int32(0)
    items_at = [(zero, zero, jnp.int32(1))]
    for n in range(ITEMS - 1):
        items_at.append(after(items_at[-1]))
    idle = ((zero, zero, zero),) * ITEMS
    lax.fori_loop(
        0,
        (items + ITEMS - 1) // ITEMS + 2,
        turn,
        (jnp.full((1, 2 * BLOCK), NEGATIVE, F32), tuple(items_at), idle, idle),
    )


def attend(table, got, peers):
    points = got.shape[2]
    per_peer = points // BLOCK
    blocks = peers * per_peer
    return pl.pallas_call(
        functools.partial(attend_kernel, peers, per_peer),
        out_shape=jax.ShapeDtypeStruct((peers, 64, points), BF16),
        in_specs=[
            pl.BlockSpec(memory_space=pltpu.SMEM),
            pl.BlockSpec(memory_space=pltpu.VMEM),
        ],
        out_specs=pl.BlockSpec(memory_space=pltpu.VMEM),
        scratch_shapes=[
            pltpu.VMEM((blocks, 128, 2 * BLOCK), BF16),
            pltpu.VMEM((blocks, BLOCK, 128), BF16),
            pltpu.VMEM((blocks + 1, 64 + ONES, BLOCK), BF16),
            pltpu.VMEM((ITEMS, GROUP * BLOCK, 2 * BLOCK), F32),
            pltpu.VMEM((ITEMS, GROUP * BLOCK, 2 * BLOCK), BF16),
            pltpu.VMEM((ITEMS, 8, 2 * BLOCK), F32),
            pltpu.VMEM((ITEMS, 8, 2 * BLOCK), F32),
            pltpu.VMEM((64 + ONES, 2 * BLOCK), F32),
        ],
        compiler_params=pltpu.CompilerParams(vmem_limit_bytes=40 << 20),
        name="attend",
    )(table, got)


def hand_out_kernel(turned_ref, served_ref, own_ref, mixed_ref, sent_ref, anchor_ref):
    turned = turned_ref[...]
    points = turned.shape[1]
    mixed_ref[...] = flip(turned)
    requests = served_ref.shape[0]

    def picks(rows):
        at = lax.broadcasted_iota(jnp.int32, (points, rows.shape[1]), 0)
        return (at == rows).astype(F32).astype(BF16)

    for r in range(0, requests, 2):
        both = jnp.concatenate([served_ref[r : r + 1, :], served_ref[r + 1 : r + 2, :]], axis=1)
        found = dot(turned, picks(both)).astype(BF16)
        sent_ref[r] = found[:, :BLOCK]
        sent_ref[r + 1] = found[:, BLOCK:]
    anchor_ref[...] = dot(turned, picks(own_ref[...])).astype(BF16)


def hand_out(turned, served, own_rows):
    width, points = turned.shape
    requests, capacity = served.shape
    anchors = own_rows.shape[1]
    return pl.pallas_call(
        hand_out_kernel,
        out_shape=(
            jax.ShapeDtypeStruct((points, width), BF16),
            jax.ShapeDtypeStruct((requests, width, capacity), BF16),
            jax.ShapeDtypeStruct((width, anchors), BF16),
        ),
        in_specs=[pl.BlockSpec(memory_space=pltpu.VMEM)] * 3,
        out_specs=[pl.BlockSpec(memory_space=pltpu.VMEM)] * 3,
        compiler_params=pltpu.CompilerParams(vmem_limit_bytes=40 << 20),
        name="hand_out",
    )(turned, served, own_rows)


def contrast_kernel(
    cand_ref, anchor_ref, weight_ref, slot_ref, live_ref, away_ref, kept_ref, embed, unit, inverse,
    expo, slopes, pulls, own_pulls
):
    pieces, width, capacity = cand_ref.shape
    anchors = anchor_ref.shape[1]
    span = 2 * capacity
    steps = pieces // 2
    turned_weight = flip(weight_ref[...])

    def normalise(rows):
        e = dot(turned_weight, rows)
        inv = lax.rsqrt(jnp.sum(e * e, axis=0, keepdims=True) + 1e-06)
        return e, inv, (e * inv).astype(BF16)

    def back(e, inv, g):
        inner = jnp.sum(e * g, axis=0, keepdims=True)
        return (inv * g - e * (inv * inv * inv * inner)).astype(BF16)

    def rows_of(i):
        return jnp.concatenate([cand_ref[2 * i], cand_ref[2 * i + 1]], axis=1)

    own = anchor_ref[...]
    own_embed, own_inverse, own_unit = normalise(own)
    own_rows = flip(own_unit)

    def column(row):
        return flip(jnp.broadcast_to(row.astype(F32), (128, anchors)))[:, :1]

    slot = column(slot_ref[...])
    live = column(live_ref[...])
    position = lax.broadcasted_iota(jnp.int32, (anchors, span), 1).astype(F32)
    sharpness = 1.0 / SHARPNESS_SCALE

    total = jnp.zeros((anchors, capacity), F32)
    right = jnp.zeros((anchors, capacity), F32)
    def take(i, e):
        at = slice(i * span, (i + 1) * span)
        inv = lax.rsqrt(jnp.sum(e * e, axis=0, keepdims=True) + 1e-06)
        embed[:, at] = e
        unit[:, at] = (e * inv).astype(BF16)
        inverse[:, at] = jnp.broadcast_to(inv, (8, span))

    def judge(i, score, total, right):
        at = slice(i * span, (i + 1) * span)
        hit = position == slot - float(i * span)
        kept = jnp.where(hit, score, 0.0)
        right = right + (kept[:, :capacity] + kept[:, capacity:])
        grown = jnp.exp2(score * (sharpness * LOG2E))
        expo[:, at] = grown
        return total + (grown[:, :capacity] + grown[:, capacity:]), right

    e = dot(turned_weight, rows_of(0))
    for i in range(steps):
        following = dot(turned_weight, rows_of(i + 1)) if i + 1 < steps else None
        take(i, e)
        e = following
        if i > 0:
            score = dot(own_rows, unit[:, (i - 1) * span : i * span])
            total, right = judge(i - 1, score, total, right)
    score = dot(own_rows, unit[:, (steps - 1) * span :])
    total, right = judge(steps - 1, score, total, right)
    total = jnp.sum(total, axis=1, keepdims=True)
    right = jnp.sum(right, axis=1, keepdims=True) * sharpness
    loss = jnp.sum(live * (jnp.log(total) - right), axis=0, keepdims=True)
    count = jnp.sum(live, axis=0, keepdims=True)
    sums = four_rows(loss, count)
    share = live / total * sharpness
    push = live * sharpness

    def slope(i):
        at = slice(i * span, (i + 1) * span)
        hit = position == slot - float(i * span)
        d = (expo[:, at] * share - jnp.where(hit, push, 0.0)).astype(BF16)
        slopes[:, at] = d
        return dot(own_unit, d)

    g = slope(0)
    for i in range(steps):
        at = slice(i * span, (i + 1) * span)
        following = slope(i + 1) if i + 1 < steps else None
        part = dot_nt(unit[:, at], slopes[:, at])
        own_grads = part if i == 0 else own_grads + part
        pulls[:, at] = back(embed[:, at], inverse[0:1, at], g)
        g = following
    own_pulls[...] = back(own_embed, own_inverse, own_grads)
    taken = jnp.concatenate([cand_ref[n] for n in range(pieces)], axis=1)
    ways = kept_ref.shape[0]
    rows = width // ways
    half = width // 2
    core = lax.rem(lax.axis_index("seq"), 2)
    for out_ref, mine in ((away_ref, 1 - core), (kept_ref, core)):
        at = pl.ds(pl.multiple_of(mine * half, half), half)
        grad = dot_nt(taken, pulls[at, :])
        grad = (grad + dot_nt(own, own_pulls[at, :])).astype(BF16)
        for j in range(ways):
            for m in range(half // 128):
                out_ref[j, m * rows : (m + 1) * rows, :] = grad[
                    j * rows : (j + 1) * rows, m * 128 : (m + 1) * 128
                ]
            out_ref[j, rows * half // 128 :, :] = sums


def contrast(candidates, anchors, weight, slot, live, ways):
    pieces, width, capacity = candidates.shape
    count = anchors.shape[1]
    many = pieces * capacity
    half = jax.ShapeDtypeStruct((ways, width * width // 2 // ways // 128 + 8, 128), BF16)
    return pl.pallas_call(
        contrast_kernel,
        out_shape=(half,) * 2,
        in_specs=[pl.BlockSpec(memory_space=pltpu.VMEM)] * 5,
        out_specs=[pl.BlockSpec(memory_space=pltpu.VMEM)] * 2,
        scratch_shapes=[
            pltpu.VMEM((width, many), F32),
            pltpu.VMEM((width, many), BF16),
            pltpu.VMEM((8, many), F32),
            pltpu.VMEM((count, many), F32),
            pltpu.VMEM((count, many), BF16),
            pltpu.VMEM((width, many), BF16),
            pltpu.VMEM((width, count), BF16),
        ],
        compiler_params=pltpu.CompilerParams(vmem_limit_bytes=48 << 20),
        name="contrast",
    )(candidates, anchors, weight, slot, live)


def summed(got_ref):
    total = got_ref[0].astype(F32)
    for n in range(1, got_ref.shape[0]):
        total += got_ref[n].astype(F32)
    part, sums = total[:-8], total[-8:]
    return part, sums[0:1] + sums[2:3], sums[1:2] + sums[3:4]


def first_sum_kernel(got_ref, out_ref):
    part, loss, count = summed(got_ref)
    rows = part.shape[0]
    part = part.astype(BF16)
    sums = four_rows(loss, count)
    for n in range(out_ref.shape[0]):
        out_ref[n, :rows, :] = part
        out_ref[n, rows:, :] = sums


def last_sum_kernel(got_ref, out_ref, loss_ref):
    part, loss, count = summed(got_ref)
    rows = out_ref.shape[1]
    part = part.astype(BF16)
    whole = jnp.concatenate(
        [part[at : at + rows, :] for at in range(0, part.shape[0], rows)], axis=1
    )
    for n in range(out_ref.shape[0]):
        out_ref[n] = whole
    loss_ref[...] = loss / count


def core_sum_kernel(one_ref, two_ref, out_ref):
    rows = out_ref.shape[1] - 8
    total = one_ref[:, :rows, :].astype(F32) + two_ref[:, :rows, :].astype(F32)
    sums = one_ref[0, rows:, :].astype(F32) + two_ref[0, rows:, :].astype(F32)
    sums = four_rows(sums[0:1] + sums[2:3], sums[1:2] + sums[3:4])
    out_ref[:, :rows, :] = total.astype(BF16)
    for n in range(out_ref.shape[0]):
        out_ref[n, rows:, :] = sums


def groups():
    close = lax.axis_size(("view", "seq"))
    events = lax.axis_size("event")
    deep = EVENT_RUN if events % EVENT_RUN == 0 else events
    planes = [
        [
            near * events + far * deep + z
            for near in range(core, close, 2)
            for far in range(events // deep)
        ]
        for core in range(2)
        for z in range(deep)
    ]
    lines = [[far * deep + z for z in range(deep)] for far in range(events // deep)]
    return planes, lines


def to_other_core(x):
    peers = lax.axis_size("seq")
    return lax.ppermute(x, "seq", [(i, i ^ 1) for i in range(peers)])


def small(kernel, name, out_shape, *operands):
    vmem = pl.BlockSpec(memory_space=pltpu.VMEM)
    return pl.pallas_call(
        kernel,
        out_shape=out_shape,
        in_specs=[vmem] * len(operands),
        out_specs=jax.tree.map(lambda shape: vmem, out_shape),
        compiler_params=pltpu.CompilerParams(vmem_limit_bytes=12 << 20),
        name=name,
    )(*operands)


def total_over_devices(away, kept, core, width):
    planes, lines = groups()
    everywhere = ("view", "seq", "event")
    ways, half = len(planes[0]), width // 2
    shape = kept.shape
    parts = small(
        core_sum_kernel, "core_sum", jax.ShapeDtypeStruct(shape, BF16), kept, to_other_core(away)
    )
    got = lax.all_to_all(parts, everywhere, 0, 0, axis_index_groups=planes, tiled=True)
    whole = small(
        first_sum_kernel, "first_sum", jax.ShapeDtypeStruct((len(lines[0]),) + shape[1:], BF16), got
    )
    got = lax.all_to_all(whole, "event", 0, 0, axis_index_groups=lines, tiled=True)
    whole, loss = small(
        last_sum_kernel,
        "last_sum",
        (
            jax.ShapeDtypeStruct((ways, width // ways, half), BF16),
            jax.ShapeDtypeStruct((1, 128), F32),
        ),
        got,
    )
    mine = lax.all_to_all(whole, everywhere, 0, 0, axis_index_groups=planes, tiled=True)
    mine = mine.reshape(width, half)
    other = to_other_core(mine)
    grad = jnp.where(
        core == 0,
        jnp.concatenate([mine, other], axis=1),
        jnp.concatenate([other, mine], axis=1),
    )
    return grad.astype(F32), loss[0, 0]


def per_device(
    query, key, value, pattern, out_weight, served, anchor_rows, positive_slot, anchor_live
):
    points, width = query.shape[2:]
    peers = lax.axis_size("seq")
    rows = pattern.shape[2]
    sent = pack(query[0, 0], key[0, 0], value[0, 0], pattern[0, 0][:, None, :], peers)
    sent, core = lax.optimization_barrier((sent, lax.rem(lax.axis_index("seq"), 2)))
    got = lax.all_to_all(sent, "seq", 0, 0, tiled=True)
    part = 3 * (width // peers)
    table = got[:, part : part + rows, :LIST].astype(jnp.int32).reshape(peers * rows, LIST)
    turned = attend(table, got, peers)
    turned = lax.all_to_all(turned, "seq", 0, 0, tiled=True).reshape(width, points)
    mixed, outgoing, anchors = hand_out(turned, served[0, 0], anchor_rows[0])
    incoming = lax.all_to_all(outgoing, ("view", "seq"), 0, 0, tiled=True)
    ways = len(groups()[0][0])
    away, kept = contrast(
        incoming, anchors, out_weight, positive_slot[0], anchor_live[0], ways
    )
    grad_total, loss = total_over_devices(away, kept, core, width)
    return (mixed[None, None], grad_total, loss)


def solution(mesh):
    placed = (
        P("event", "view", "seq", None),
        P("event", "view", "seq", None),
        P("event", "view", "seq", None),
        P("event", "view", "seq", None),
        P(),
        P("event", "view", "seq", None),
        P("event", "view", "seq"),
        P("event", "view", "seq"),
        P("event", "view", "seq"),
    )
    return jax.shard_map(
        per_device,
        mesh=mesh,
        in_specs=placed,
        out_specs=(P("event", "view", "seq", None), P(), P()),
        check_vma=False,
    )
```

```python
import functools

import jax
import jax.numpy as jnp
from jax import lax
from jax.experimental import pallas as pl
from jax.experimental.pallas import tpu as pltpu
from jax.sharding import PartitionSpec as P

HEADS = 16
BLOCK = 128
SHARPNESS_SCALE = 0.07
GROUP = 2
ITEMS = 6
EXTRA = 8
ONES = 16
EVENT_RUN = 8
LIST = 32
NEGATIVE = -1e30
LOG2E = 1.4426950408889634

F32 = jnp.float32
BF16 = jnp.bfloat16


def dot(a, b):
    return lax.dot_general(a, b, (((1,), (0,)), ((), ())), preferred_element_type=F32)


def dot_nt(a, b):
    return lax.dot_general(a, b, (((1,), (1,)), ((), ())), preferred_element_type=F32)


def flip(x):
    return jnp.transpose(x, (1, 0))


def pack_kernel(
    peers, rows, q_hbm, k_hbm, v_hbm, pattern_hbm, out_ref, q_ref, k_ref, v_ref, pattern_ref, sems
):
    points, full = q_ref.shape
    width = full // peers
    spans = [slice(at, at + BLOCK) for at in range(0, points, BLOCK)]
    copies = [pltpu.make_async_copy(pattern_hbm, pattern_ref, sems.at[0])]
    for n, (source, target) in enumerate(((v_hbm, v_ref), (q_hbm, q_ref), (k_hbm, k_ref))):
        for m, span in enumerate(spans):
            copies.append(
                pltpu.make_async_copy(
                    source.at[span, :], target.at[span, :], sems.at[1 + n * len(spans) + m]
                )
            )
    for copy in copies:
        copy.start()

    copies[0].wait()
    blocks = pattern_ref.shape[2]
    allowed = jnp.concatenate([pattern_ref[r] for r in range(rows)], axis=0)
    allowed = (allowed > 0).astype(F32)
    before = lax.broadcasted_iota(jnp.int32, (blocks, blocks), 0)
    after = lax.broadcasted_iota(jnp.int32, (blocks, blocks), 1)
    rank = dot(allowed.astype(BF16), (before <= after).astype(BF16)) - 1.0
    place = lax.broadcasted_iota(jnp.int32, (LIST, blocks), 0).astype(F32)
    number = lax.broadcasted_iota(jnp.int32, (LIST, blocks), 1).astype(F32)
    lane = lax.broadcasted_iota(jnp.int32, (LIST, 128), 1)
    table = jnp.zeros((LIST, 128), F32)
    for r in range(rows):
        on = allowed[r : r + 1, :]
        count = jnp.sum(on, axis=1, keepdims=True)
        here = jnp.where(place < count, place, 0.0)
        hit = jnp.where(rank[r : r + 1, :] == here, on, 0.0)
        column = jnp.sum(hit * number, axis=1, keepdims=True)
        column = jnp.where(place[:, :1] == float(blocks), count, column)
        table = jnp.where(lane == r, column, table)
    lists = flip(table)[:EXTRA, :].astype(BF16)
    tail = jnp.concatenate(
        [lists, jnp.zeros((EXTRA, 128 - LIST), BF16)]
        + [jnp.zeros((EXTRA, 128), BF16)] * (points // 128 - 1),
        axis=1,
    )
    for j in range(peers):
        out_ref[j, 3 * width : 3 * width + EXTRA, :] = tail

    for n, (at, ref) in enumerate(((2, v_ref), (0, q_ref))):
        for m, span in enumerate(spans):
            copies[1 + n * len(spans) + m].wait()
            turned = flip(ref[span, :])
            for j in range(peers):
                out_ref[j, at * width : (at + 1) * width, span] = turned[
                    j * width : (j + 1) * width, :
                ]
    for m, span in enumerate(spans):
        copies[1 + 2 * len(spans) + m].wait()
        for j in range(peers):
            cols = slice(j * width, (j + 1) * width)
            first = k_ref[span.start : span.start + width, cols]
            second = k_ref[span.start + width : span.stop, cols]
            out_ref[j, width : 2 * width, span] = jnp.concatenate([first, second], axis=1)


def pack(queries, keys, values, pattern, peers):
    points, width = queries.shape
    rows = 3 * (width // peers) + EXTRA
    return pl.pallas_call(
        functools.partial(pack_kernel, peers, pattern.shape[0]),
        out_shape=jax.ShapeDtypeStruct((peers, rows, points), BF16),
        in_specs=[pl.BlockSpec(memory_space=pltpu.HBM)] * 4,
        out_specs=pl.BlockSpec(memory_space=pltpu.VMEM),
        scratch_shapes=[
            pltpu.VMEM((points, width), BF16),
            pltpu.VMEM((points, width), BF16),
            pltpu.VMEM((points, width), BF16),
            pltpu.VMEM(pattern.shape, jnp.int32),
            pltpu.SemaphoreType.DMA((1 + 3 * (points // BLOCK),)),
        ],
        compiler_params=pltpu.CompilerParams(vmem_limit_bytes=16 << 20),
        name="pack_heads",
    )(*(pltpu.with_memory_space_constraint(x, pltpu.HBM) for x in (queries, keys, values, pattern)))


def four_rows(first, second):
    row = lax.broadcasted_iota(jnp.int32, (8, 128), 0)
    value = jnp.where(lax.rem(row, 2) == 0, first, second)
    high = value.astype(BF16).astype(F32)
    return jnp.where(row < 2, high, jnp.where(row < 4, value - high, 0.0)).astype(BF16)


def attend_kernel(
    peers, per_peer, table_ref, got_ref, out_ref, qb, kb, vb, scored, weighed, peak, fade, accum
):
    blocks = peers * per_peer
    head = 32
    factor = head ** (-0.5) * LOG2E
    zero = jnp.zeros((head, BLOCK), BF16)
    ones = (lax.broadcasted_iota(jnp.int32, (ONES, BLOCK), 0) == 0).astype(F32).astype(BF16)

    for j in range(peers):
        for b in range(per_peer):
            block = j * per_peer + b
            span = slice(b * BLOCK, (b + 1) * BLOCK)
            scaled = got_ref[j, 0 : 2 * head, span].astype(F32) * factor
            high = scaled.astype(BF16)
            low = (scaled - high.astype(F32)).astype(BF16)
            left = jnp.concatenate([high[:head], zero, low[:head], zero], axis=0)
            right = jnp.concatenate([zero, high[head:], zero, low[head:]], axis=0)
            qb[block, :, 0:BLOCK] = left
            qb[block, :, BLOCK : 2 * BLOCK] = right
            pair = got_ref[j, 2 * head : 4 * head, span]
            first, second = pair[:, : 2 * head], pair[:, 2 * head :]
            kb[block, : BLOCK // 2, :] = jnp.concatenate([first, first], axis=1)
            kb[block, BLOCK // 2 :, :] = jnp.concatenate([second, second], axis=1)
            vb[block, 0 : 2 * head, :] = got_ref[j, 4 * head : 6 * head, span]
            vb[block, 2 * head : 2 * head + ONES, :] = ones

    vb[blocks, :, :] = jnp.zeros((2 * head + ONES, BLOCK), BF16)
    steps_of = [(table_ref[i, blocks] + GROUP - 1) // GROUP for i in range(blocks)]
    items = functools.reduce(lambda x, y: x + y, steps_of)

    def after(item):
        row, step, real = item
        last = (step + 1) * GROUP >= table_ref[row, blocks]
        end = jnp.logical_and(last, row == blocks - 1)
        return (
            jnp.where(jnp.logical_and(last, row < blocks - 1), row + 1, row),
            jnp.where(end, step, jnp.where(last, 0, step + 1)),
            jnp.where(end, 0, real),
        )

    def turn(t, carry):
        best, at_scores, at_weights, at_sums = carry
        total = jnp.where(t < 3, 0.0, accum[...])
        for n, (row, step, real) in enumerate(at_sums):
            first = step * GROUP
            count = jnp.where(real == 1, table_ref[row, blocks], 0)
            picked = []
            for g in range(GROUP):
                picked.append(vb[jnp.where(first + g < count, table_ref[row, first + g], blocks)])
            added = dot(jnp.concatenate(picked, axis=1), weighed[n])
            total = total * fade[n, 0:1, :] + added
            share = pl.reciprocal(total[2 * head : 2 * head + 1, :])
            j, b = row // per_peer, lax.rem(row, per_peer)
            span = pl.ds(pl.multiple_of(b * BLOCK, BLOCK), BLOCK)
            out_ref[j, 0:head, span] = (total[0:head, 0:BLOCK] * share[:, 0:BLOCK]).astype(BF16)
            out_ref[j, head : 2 * head, span] = (
                total[head : 2 * head, BLOCK : 2 * BLOCK] * share[:, BLOCK : 2 * BLOCK]
            ).astype(BF16)
        accum[...] = total
        for n, (row, step, real) in enumerate(at_weights):
            best = jnp.where(jnp.logical_and(step == 0, real == 1), NEGATIVE, best)
            new_best = jnp.maximum(best, peak[n, 0:1, :])
            weighed[n] = jnp.exp2(scored[n] - new_best).astype(BF16)
            fade[n] = jnp.broadcast_to(jnp.exp2(best - new_best), (8, 2 * BLOCK))
            best = new_best
        for n, (row, step, real) in enumerate(at_scores):
            picked = [kb[table_ref[row, step * GROUP + g]] for g in range(GROUP)]
            scores = dot(jnp.concatenate(picked, axis=0), qb[row])
            scored[n] = scores
            top = jnp.max(scores.reshape(GROUP * BLOCK // 8, 8, 2 * BLOCK), axis=0)
            peak[n] = jnp.broadcast_to(jnp.max(top, axis=0, keepdims=True), (8, 2 * BLOCK))
        following = [after(at_scores[-1])]
        for n in range(ITEMS - 1):
            following.append(after(following[-1]))
        return best, tuple(following), at_scores, at_weights

    zero = jnp.int32(0)
    items_at = [(zero, zero, jnp.int32(1))]
    for n in range(ITEMS - 1):
        items_at.append(after(items_at[-1]))
    idle = ((zero, zero, zero),) * ITEMS
    lax.fori_loop(
        0,
        (items + ITEMS - 1) // ITEMS + 2,
        turn,
        (jnp.full((1, 2 * BLOCK), NEGATIVE, F32), tuple(items_at), idle, idle),
    )


def attend(table, got, peers):
    points = got.shape[2]
    per_peer = points // BLOCK
    blocks = peers * per_peer
    return pl.pallas_call(
        functools.partial(attend_kernel, peers, per_peer),
        out_shape=jax.ShapeDtypeStruct((peers, 64, points), BF16),
        in_specs=[
            pl.BlockSpec(memory_space=pltpu.SMEM),
            pl.BlockSpec(memory_space=pltpu.VMEM),
        ],
        out_specs=pl.BlockSpec(memory_space=pltpu.VMEM),
        scratch_shapes=[
            pltpu.VMEM((blocks, 128, 2 * BLOCK), BF16),
            pltpu.VMEM((blocks, BLOCK, 128), BF16),
            pltpu.VMEM((blocks + 1, 64 + ONES, BLOCK), BF16),
            pltpu.VMEM((ITEMS, GROUP * BLOCK, 2 * BLOCK), F32),
            pltpu.VMEM((ITEMS, GROUP * BLOCK, 2 * BLOCK), BF16),
            pltpu.VMEM((ITEMS, 8, 2 * BLOCK), F32),
            pltpu.VMEM((ITEMS, 8, 2 * BLOCK), F32),
            pltpu.VMEM((64 + ONES, 2 * BLOCK), F32),
        ],
        compiler_params=pltpu.CompilerParams(vmem_limit_bytes=40 << 20),
        name="attend",
    )(table, got)


def hand_out_kernel(
    turned_ref, served_ref, own_ref, mixed_hbm, sent_ref, anchor_ref, mixed_ref, sem
):
    turned = turned_ref[...]
    points = turned.shape[1]
    mixed_ref[...] = flip(turned)
    leaving = pltpu.make_async_copy(mixed_ref, mixed_hbm, sem.at[0])
    leaving.start()
    requests = served_ref.shape[0]

    def picks(rows):
        at = lax.broadcasted_iota(jnp.int32, (points, rows.shape[1]), 0)
        return (at == rows).astype(F32).astype(BF16)

    for r in range(0, requests, 2):
        both = jnp.concatenate([served_ref[r : r + 1, :], served_ref[r + 1 : r + 2, :]], axis=1)
        found = dot(turned, picks(both)).astype(BF16)
        sent_ref[r] = found[:, :BLOCK]
        sent_ref[r + 1] = found[:, BLOCK:]
    anchor_ref[...] = dot(turned, picks(own_ref[...])).astype(BF16)
    leaving.wait()


def hand_out(turned, served, own_rows):
    width, points = turned.shape
    requests, capacity = served.shape
    anchors = own_rows.shape[1]
    return pl.pallas_call(
        hand_out_kernel,
        out_shape=(
            jax.ShapeDtypeStruct((points, width), BF16),
            jax.ShapeDtypeStruct((requests, width, capacity), BF16),
            jax.ShapeDtypeStruct((width, anchors), BF16),
        ),
        in_specs=[pl.BlockSpec(memory_space=pltpu.VMEM)] * 3,
        out_specs=[
            pl.BlockSpec(memory_space=pl.ANY),
            pl.BlockSpec(memory_space=pltpu.VMEM),
            pl.BlockSpec(memory_space=pltpu.VMEM),
        ],
        scratch_shapes=[pltpu.VMEM((points, width), BF16), pltpu.SemaphoreType.DMA((1,))],
        compiler_params=pltpu.CompilerParams(vmem_limit_bytes=40 << 20),
        name="hand_out",
    )(turned, served, own_rows)


def contrast_kernel(
    cand_ref, anchor_ref, weight_ref, slot_ref, live_ref, away_ref, pulls,
    own_pulls, embed, unit, inverse,
    expo, slopes
):
    pieces, width, capacity = cand_ref.shape
    anchors = anchor_ref.shape[1]
    span = 2 * capacity
    steps = pieces // 2
    turned_weight = flip(weight_ref[...])

    def normalise(rows):
        e = dot(turned_weight, rows)
        inv = lax.rsqrt(jnp.sum(e * e, axis=0, keepdims=True) + 1e-06)
        return e, inv, (e * inv).astype(BF16)

    def back(e, inv, g):
        inner = jnp.sum(e * g, axis=0, keepdims=True)
        return (inv * g - e * (inv * inv * inv * inner)).astype(BF16)

    def rows_of(i):
        return jnp.concatenate([cand_ref[2 * i], cand_ref[2 * i + 1]], axis=1)

    own = anchor_ref[...]
    own_embed, own_inverse, own_unit = normalise(own)
    own_rows = flip(own_unit)

    def column(row):
        return flip(jnp.broadcast_to(row.astype(F32), (128, anchors)))[:, :1]

    slot = column(slot_ref[...])
    live = column(live_ref[...])
    position = lax.broadcasted_iota(jnp.int32, (anchors, span), 1).astype(F32)
    sharpness = 1.0 / SHARPNESS_SCALE

    total = jnp.zeros((anchors, capacity), F32)
    right = jnp.zeros((anchors, capacity), F32)
    def take(i, e):
        at = slice(i * span, (i + 1) * span)
        inv = lax.rsqrt(jnp.sum(e * e, axis=0, keepdims=True) + 1e-06)
        embed[:, at] = e
        unit[:, at] = (e * inv).astype(BF16)
        inverse[:, at] = jnp.broadcast_to(inv, (8, span))

    def judge(i, score, total, right):
        at = slice(i * span, (i + 1) * span)
        hit = position == slot - float(i * span)
        kept = jnp.where(hit, score, 0.0)
        right = right + (kept[:, :capacity] + kept[:, capacity:])
        grown = jnp.exp2(score * (sharpness * LOG2E))
        expo[:, at] = grown
        return total + (grown[:, :capacity] + grown[:, capacity:]), right

    e = dot(turned_weight, rows_of(0))
    for i in range(steps):
        following = dot(turned_weight, rows_of(i + 1)) if i + 1 < steps else None
        take(i, e)
        e = following
        if i > 0:
            score = dot(own_rows, unit[:, (i - 1) * span : i * span])
            total, right = judge(i - 1, score, total, right)
    score = dot(own_rows, unit[:, (steps - 1) * span :])
    total, right = judge(steps - 1, score, total, right)
    total = jnp.sum(total, axis=1, keepdims=True)
    right = jnp.sum(right, axis=1, keepdims=True) * sharpness
    loss = jnp.sum(live * (jnp.log(total) - right), axis=0, keepdims=True)
    count = jnp.sum(live, axis=0, keepdims=True)
    sums = four_rows(loss, count)
    share = live / total * sharpness
    push = live * sharpness

    def slope(i):
        at = slice(i * span, (i + 1) * span)
        hit = position == slot - float(i * span)
        d = (expo[:, at] * share - jnp.where(hit, push, 0.0)).astype(BF16)
        slopes[:, at] = d
        return dot(own_unit, d)

    g = slope(0)
    for i in range(steps):
        at = slice(i * span, (i + 1) * span)
        following = slope(i + 1) if i + 1 < steps else None
        part = dot_nt(unit[:, at], slopes[:, at])
        own_grads = part if i == 0 else own_grads + part
        pulls[:, at] = back(embed[:, at], inverse[0:1, at], g)
        g = following
    own_pulls[...] = back(own_embed, own_inverse, own_grads)
    core = lax.rem(lax.axis_index("seq"), 2)
    half_of_gradient(1 - core, cand_ref, own, pulls, own_pulls, sums, away_ref)


def half_of_gradient(mine, cand_ref, own, pulls, own_pulls, sums, out_ref):
    pieces, width = cand_ref.shape[:2]
    ways = out_ref.shape[0]
    rows, half = width // ways, width // 2
    taken = jnp.concatenate([cand_ref[n] for n in range(pieces)], axis=1)
    at = pl.ds(pl.multiple_of(mine * half, half), half)
    grad = dot_nt(taken, pulls[at, :])
    grad = (grad + dot_nt(own, own_pulls[at, :])).astype(BF16)
    for j in range(ways):
        for m in range(half // 128):
            out_ref[j, m * rows : (m + 1) * rows, :] = grad[
                j * rows : (j + 1) * rows, m * 128 : (m + 1) * 128
            ]
        out_ref[j, rows * half // 128 :, :] = sums


def keep_kernel(cand_ref, anchor_ref, pulls_ref, own_pulls_ref, away_ref, kept_ref):
    core = lax.rem(lax.axis_index("seq"), 2)
    sums = away_ref[0, away_ref.shape[1] - 8 :, :]
    half_of_gradient(core, cand_ref, anchor_ref[...], pulls_ref, own_pulls_ref, sums, kept_ref)


def keep(candidates, anchors, pulls, own_pulls, away):
    vmem = pl.BlockSpec(memory_space=pltpu.VMEM)
    width, many = pulls.shape
    return pl.pallas_call(
        keep_kernel,
        out_shape=jax.ShapeDtypeStruct(away.shape, BF16),
        in_specs=[vmem] * 5,
        out_specs=vmem,
        compiler_params=pltpu.CompilerParams(vmem_limit_bytes=16 << 20),
        cost_estimate=pl.CostEstimate(
            flops=width * width * many, bytes_accessed=4 * width * many, transcendentals=0
        ),
        name="keep",
    )(candidates, anchors, pulls, own_pulls, away)


def contrast(candidates, anchors, weight, slot, live, ways):
    pieces, width, capacity = candidates.shape
    count = anchors.shape[1]
    many = pieces * capacity
    half = jax.ShapeDtypeStruct((ways, width * width // 2 // ways // 128 + 8, 128), BF16)
    return pl.pallas_call(
        contrast_kernel,
        out_shape=(
            half,
            jax.ShapeDtypeStruct((width, many), BF16),
            jax.ShapeDtypeStruct((width, count), BF16),
        ),
        in_specs=[pl.BlockSpec(memory_space=pltpu.VMEM)] * 5,
        out_specs=[pl.BlockSpec(memory_space=pltpu.VMEM)] * 3,
        scratch_shapes=[
            pltpu.VMEM((width, many), F32),
            pltpu.VMEM((width, many), BF16),
            pltpu.VMEM((8, many), F32),
            pltpu.VMEM((count, many), F32),
            pltpu.VMEM((count, many), BF16),
        ],
        compiler_params=pltpu.CompilerParams(vmem_limit_bytes=28 << 20),
        name="contrast",
    )(candidates, anchors, weight, slot, live)


def summed(got_ref):
    total = got_ref[0].astype(F32)
    for n in range(1, got_ref.shape[0]):
        total += got_ref[n].astype(F32)
    part, sums = total[:-8], total[-8:]
    return part, sums[0:1] + sums[2:3], sums[1:2] + sums[3:4]


def first_sum_kernel(got_ref, out_ref):
    part, loss, count = summed(got_ref)
    rows = part.shape[0]
    part = part.astype(BF16)
    sums = four_rows(loss, count)
    for n in range(out_ref.shape[0]):
        out_ref[n, :rows, :] = part
        out_ref[n, rows:, :] = sums


def last_sum_kernel(got_ref, out_ref, loss_ref):
    part, loss, count = summed(got_ref)
    rows = out_ref.shape[1]
    part = part.astype(BF16)
    whole = jnp.concatenate(
        [part[at : at + rows, :] for at in range(0, part.shape[0], rows)], axis=1
    )
    for n in range(out_ref.shape[0]):
        out_ref[n] = whole
    loss_ref[...] = loss / count


def core_sum_kernel(one_ref, two_ref, out_ref):
    rows = out_ref.shape[1] - 8
    total = one_ref[:, :rows, :].astype(F32) + two_ref[:, :rows, :].astype(F32)
    sums = one_ref[0, rows:, :].astype(F32) + two_ref[0, rows:, :].astype(F32)
    sums = four_rows(sums[0:1] + sums[2:3], sums[1:2] + sums[3:4])
    out_ref[:, :rows, :] = total.astype(BF16)
    for n in range(out_ref.shape[0]):
        out_ref[n, rows:, :] = sums


def groups():
    close = lax.axis_size(("view", "seq"))
    events = lax.axis_size("event")
    deep = EVENT_RUN if events % EVENT_RUN == 0 else events
    planes = [
        [
            near * events + far * deep + z
            for near in range(core, close, 2)
            for far in range(events // deep)
        ]
        for core in range(2)
        for z in range(deep)
    ]
    lines = [[far * deep + z for z in range(deep)] for far in range(events // deep)]
    return planes, lines


def to_other_core(x):
    peers = lax.axis_size("seq")
    return lax.ppermute(x, "seq", [(i, i ^ 1) for i in range(peers)])


def small(kernel, name, out_shape, *operands):
    vmem = pl.BlockSpec(memory_space=pltpu.VMEM)
    return pl.pallas_call(
        kernel,
        out_shape=out_shape,
        in_specs=[vmem] * len(operands),
        out_specs=jax.tree.map(lambda shape: vmem, out_shape),
        compiler_params=pltpu.CompilerParams(vmem_limit_bytes=12 << 20),
        name=name,
    )(*operands)


def total_over_devices(received, kept, core, width):
    planes, lines = groups()
    everywhere = ("view", "seq", "event")
    ways, half = len(planes[0]), width // 2
    shape = kept.shape
    parts = small(
        core_sum_kernel, "core_sum", jax.ShapeDtypeStruct(shape, BF16), kept, received
    )
    got = lax.all_to_all(parts, everywhere, 0, 0, axis_index_groups=planes, tiled=True)
    whole = small(
        first_sum_kernel, "first_sum", jax.ShapeDtypeStruct((len(lines[0]),) + shape[1:], BF16), got
    )
    got = lax.all_to_all(whole, "event", 0, 0, axis_index_groups=lines, tiled=True)
    whole, loss = small(
        last_sum_kernel,
        "last_sum",
        (
            jax.ShapeDtypeStruct((ways, width // ways, half), BF16),
            jax.ShapeDtypeStruct((1, 128), F32),
        ),
        got,
    )
    mine = lax.all_to_all(whole, everywhere, 0, 0, axis_index_groups=planes, tiled=True)
    mine = mine.reshape(width, half)
    other = to_other_core(mine)
    grad = jnp.where(
        core == 0,
        jnp.concatenate([mine, other], axis=1),
        jnp.concatenate([other, mine], axis=1),
    )
    return grad.astype(F32), loss[0, 0]


def per_device(
    query, key, value, pattern, out_weight, served, anchor_rows, positive_slot, anchor_live
):
    points, width = query.shape[2:]
    peers = lax.axis_size("seq")
    rows = pattern.shape[2]
    sent = pack(query[0, 0], key[0, 0], value[0, 0], pattern[0, 0][:, None, :], peers)
    sent, core = lax.optimization_barrier((sent, lax.rem(lax.axis_index("seq"), 2)))
    got = lax.all_to_all(sent, "seq", 0, 0, tiled=True)
    part = 3 * (width // peers)
    table = got[:, part : part + rows, :LIST].astype(jnp.int32).reshape(peers * rows, LIST)
    turned = attend(table, got, peers)
    turned = lax.all_to_all(turned, "seq", 0, 0, tiled=True).reshape(width, points)
    mixed, outgoing, anchors = hand_out(turned, served[0, 0], anchor_rows[0])
    incoming = lax.all_to_all(outgoing, ("view", "seq"), 0, 0, tiled=True)
    ways = len(groups()[0][0])
    away, pulls, own_pulls = contrast(
        incoming, anchors, out_weight, positive_slot[0], anchor_live[0], ways
    )
    received = to_other_core(away)
    kept = keep(incoming, anchors, pulls, own_pulls, away)
    grad_total, loss = total_over_devices(received, kept, core, width)
    return (mixed[None, None], grad_total, loss)


def solution(mesh):
    placed = (
        P("event", "view", "seq", None),
        P("event", "view", "seq", None),
        P("event", "view", "seq", None),
        P("event", "view", "seq", None),
        P(),
        P("event", "view", "seq", None),
        P("event", "view", "seq"),
        P("event", "view", "seq"),
        P("event", "view", "seq"),
    )
    return jax.shard_map(
        per_device,
        mesh=mesh,
        in_specs=placed,
        out_specs=(P("event", "view", "seq", None), P(), P()),
        check_vma=False,
    )
```

```python
import functools

import jax
import jax.numpy as jnp
from jax import lax
from jax.experimental import pallas as pl
from jax.experimental.pallas import tpu as pltpu
from jax.sharding import PartitionSpec as P

HEADS = 16
BLOCK = 128
SHARPNESS_SCALE = 0.07
GROUP = 2
ITEMS = 8
EXTRA = 8
ONES = 16
EVENT_RUN = 8
LIST = 32
NEGATIVE = -1e30
LOG2E = 1.4426950408889634

F32 = jnp.float32
BF16 = jnp.bfloat16


def dot(a, b):
    return lax.dot_general(a, b, (((1,), (0,)), ((), ())), preferred_element_type=F32)


def dot_nt(a, b):
    return lax.dot_general(a, b, (((1,), (1,)), ((), ())), preferred_element_type=F32)


def flip(x):
    return jnp.transpose(x, (1, 0))


def pack_kernel(
    peers, rows, q_hbm, k_hbm, v_hbm, pattern_hbm, out_ref, q_ref, k_ref, v_ref, pattern_ref, sems
):
    points, full = q_ref.shape
    width = full // peers
    spans = [slice(at, at + BLOCK) for at in range(0, points, BLOCK)]
    copies = [pltpu.make_async_copy(pattern_hbm, pattern_ref, sems.at[0])]
    for n, (source, target) in enumerate(((v_hbm, v_ref), (q_hbm, q_ref), (k_hbm, k_ref))):
        for m, span in enumerate(spans):
            copies.append(
                pltpu.make_async_copy(
                    source.at[span, :], target.at[span, :], sems.at[1 + n * len(spans) + m]
                )
            )
    for copy in copies:
        copy.start()

    copies[0].wait()
    blocks = pattern_ref.shape[2]
    allowed = jnp.concatenate([pattern_ref[r] for r in range(rows)], axis=0)
    allowed = (allowed > 0).astype(F32)
    before = lax.broadcasted_iota(jnp.int32, (blocks, blocks), 0)
    after = lax.broadcasted_iota(jnp.int32, (blocks, blocks), 1)
    rank = dot(allowed.astype(BF16), (before <= after).astype(BF16)) - 1.0
    place = lax.broadcasted_iota(jnp.int32, (LIST, blocks), 0).astype(F32)
    number = lax.broadcasted_iota(jnp.int32, (LIST, blocks), 1).astype(F32)
    lane = lax.broadcasted_iota(jnp.int32, (LIST, 128), 1)
    table = jnp.zeros((LIST, 128), F32)
    for r in range(rows):
        on = allowed[r : r + 1, :]
        count = jnp.sum(on, axis=1, keepdims=True)
        here = jnp.where(place < count, place, 0.0)
        hit = jnp.where(rank[r : r + 1, :] == here, on, 0.0)
        column = jnp.sum(hit * number, axis=1, keepdims=True)
        column = jnp.where(place[:, :1] == float(blocks), count, column)
        table = jnp.where(lane == r, column, table)
    lists = flip(table)[:EXTRA, :].astype(BF16)
    tail = jnp.concatenate(
        [lists, jnp.zeros((EXTRA, 128 - LIST), BF16)]
        + [jnp.zeros((EXTRA, 128), BF16)] * (points // 128 - 1),
        axis=1,
    )
    for j in range(peers):
        out_ref[j, 3 * width : 3 * width + EXTRA, :] = tail

    for n, (at, ref) in enumerate(((2, v_ref), (0, q_ref))):
        for m, span in enumerate(spans):
            copies[1 + n * len(spans) + m].wait()
            turned = flip(ref[span, :])
            for j in range(peers):
                out_ref[j, at * width : (at + 1) * width, span] = turned[
                    j * width : (j + 1) * width, :
                ]
    for m, span in enumerate(spans):
        copies[1 + 2 * len(spans) + m].wait()
        for j in range(peers):
            cols = slice(j * width, (j + 1) * width)
            first = k_ref[span.start : span.start + width, cols]
            second = k_ref[span.start + width : span.stop, cols]
            out_ref[j, width : 2 * width, span] = jnp.concatenate([first, second], axis=1)


def pack(queries, keys, values, pattern, peers):
    points, width = queries.shape
    rows = 3 * (width // peers) + EXTRA
    return pl.pallas_call(
        functools.partial(pack_kernel, peers, pattern.shape[0]),
        out_shape=jax.ShapeDtypeStruct((peers, rows, points), BF16),
        in_specs=[pl.BlockSpec(memory_space=pltpu.HBM)] * 4,
        out_specs=pl.BlockSpec(memory_space=pltpu.VMEM),
        scratch_shapes=[
            pltpu.VMEM((points, width), BF16),
            pltpu.VMEM((points, width), BF16),
            pltpu.VMEM((points, width), BF16),
            pltpu.VMEM(pattern.shape, jnp.int32),
            pltpu.SemaphoreType.DMA((1 + 3 * (points // BLOCK),)),
        ],
        compiler_params=pltpu.CompilerParams(vmem_limit_bytes=16 << 20),
        name="pack_heads",
    )(*(pltpu.with_memory_space_constraint(x, pltpu.HBM) for x in (queries, keys, values, pattern)))


def four_rows(first, second):
    row = lax.broadcasted_iota(jnp.int32, (8, 128), 0)
    value = jnp.where(lax.rem(row, 2) == 0, first, second)
    high = value.astype(BF16).astype(F32)
    return jnp.where(row < 2, high, jnp.where(row < 4, value - high, 0.0)).astype(BF16)


def attend_kernel(
    peers, per_peer, table_ref, got_ref, out_ref, qb, kb, vb, scored, weighed, peak, fade, accum
):
    blocks = peers * per_peer
    head = 32
    factor = head ** (-0.5) * LOG2E
    zero = jnp.zeros((head, BLOCK), BF16)
    ones = (lax.broadcasted_iota(jnp.int32, (ONES, BLOCK), 0) == 0).astype(F32).astype(BF16)

    for j in range(peers):
        for b in range(per_peer):
            block = j * per_peer + b
            span = slice(b * BLOCK, (b + 1) * BLOCK)
            scaled = got_ref[j, 0 : 2 * head, span].astype(F32) * factor
            high = scaled.astype(BF16)
            low = (scaled - high.astype(F32)).astype(BF16)
            left = jnp.concatenate([high[:head], zero, low[:head], zero], axis=0)
            right = jnp.concatenate([zero, high[head:], zero, low[head:]], axis=0)
            qb[block, :, 0:BLOCK] = left
            qb[block, :, BLOCK : 2 * BLOCK] = right
            pair = got_ref[j, 2 * head : 4 * head, span]
            first, second = pair[:, : 2 * head], pair[:, 2 * head :]
            kb[block, : BLOCK // 2, :] = jnp.concatenate([first, first], axis=1)
            kb[block, BLOCK // 2 :, :] = jnp.concatenate([second, second], axis=1)
            vb[block, 0 : 2 * head, :] = got_ref[j, 4 * head : 6 * head, span]
            vb[block, 2 * head : 2 * head + ONES, :] = ones

    vb[blocks, :, :] = jnp.zeros((2 * head + ONES, BLOCK), BF16)
    steps_of = [(table_ref[i, blocks] + GROUP - 1) // GROUP for i in range(blocks)]
    items = functools.reduce(lambda x, y: x + y, steps_of)

    def after(item):
        row, step, real = item
        last = (step + 1) * GROUP >= table_ref[row, blocks]
        end = jnp.logical_and(last, row == blocks - 1)
        return (
            jnp.where(jnp.logical_and(last, row < blocks - 1), row + 1, row),
            jnp.where(end, step, jnp.where(last, 0, step + 1)),
            jnp.where(end, 0, real),
        )

    def turn(t, carry, sums=True, weights=True, scores=True):
        best, at_scores, at_weights, at_sums = carry
        if sums:
            take_sums(at_sums)
        if weights:
            best = take_weights(best, at_weights)
        if not scores:
            return best, at_scores, at_scores, at_weights
        take_scores(at_scores)
        following = [after(at_scores[-1])]
        for n in range(ITEMS - 1):
            following.append(after(following[-1]))
        return best, tuple(following), at_scores, at_weights

    def take_sums(at_sums):
        total = accum[...]
        for n, (row, step, real) in enumerate(at_sums):
            first = step * GROUP
            count = jnp.where(real == 1, table_ref[row, blocks], 0)
            picked = []
            for g in range(GROUP):
                picked.append(vb[jnp.where(first + g < count, table_ref[row, first + g], blocks)])
            added = dot(jnp.concatenate(picked, axis=1), weighed[n])
            total = total * fade[n, 0:1, :] + added
            share = pl.reciprocal(total[2 * head : 2 * head + 1, :])
            j, b = row // per_peer, lax.rem(row, per_peer)
            span = pl.ds(pl.multiple_of(b * BLOCK, BLOCK), BLOCK)
            out_ref[j, 0:head, span] = (total[0:head, 0:BLOCK] * share[:, 0:BLOCK]).astype(BF16)
            out_ref[j, head : 2 * head, span] = (
                total[head : 2 * head, BLOCK : 2 * BLOCK] * share[:, BLOCK : 2 * BLOCK]
            ).astype(BF16)
        accum[...] = total

    def take_weights(best, at_weights):
        for n, (row, step, real) in enumerate(at_weights):
            best = jnp.where(jnp.logical_and(step == 0, real == 1), NEGATIVE, best)
            new_best = jnp.maximum(best, peak[n, 0:1, :])
            weighed[n] = jnp.exp2(scored[n] - new_best).astype(BF16)
            fade[n] = jnp.broadcast_to(jnp.exp2(best - new_best), (8, 2 * BLOCK))
            best = new_best
        return best

    def take_scores(at_scores):
        for n, (row, step, real) in enumerate(at_scores):
            picked = [kb[table_ref[row, step * GROUP + g]] for g in range(GROUP)]
            scores = dot(jnp.concatenate(picked, axis=0), qb[row])
            scored[n] = scores
            top = jnp.max(scores.reshape(GROUP * BLOCK // 8, 8, 2 * BLOCK), axis=0)
            peak[n] = jnp.broadcast_to(jnp.max(top, axis=0, keepdims=True), (8, 2 * BLOCK))

    zero = jnp.int32(0)
    items_at = [(zero, zero, jnp.int32(1))]
    for n in range(ITEMS - 1):
        items_at.append(after(items_at[-1]))
    idle = ((zero, zero, zero),) * ITEMS
    accum[...] = jnp.zeros_like(accum)
    carry = (jnp.full((1, 2 * BLOCK), NEGATIVE, F32), tuple(items_at), idle, idle)
    carry = turn(0, carry, sums=False, weights=False)
    carry = turn(1, carry, sums=False)
    carry = lax.fori_loop(2, (items + ITEMS - 1) // ITEMS, turn, carry)
    carry = turn(0, carry, scores=False)
    turn(0, carry, weights=False, scores=False)


def attend(table, got, peers):
    points = got.shape[2]
    per_peer = points // BLOCK
    blocks = peers * per_peer
    return pl.pallas_call(
        functools.partial(attend_kernel, peers, per_peer),
        out_shape=jax.ShapeDtypeStruct((peers, 64, points), BF16),
        in_specs=[
            pl.BlockSpec(memory_space=pltpu.SMEM),
            pl.BlockSpec(memory_space=pltpu.VMEM),
        ],
        out_specs=pl.BlockSpec(memory_space=pltpu.VMEM),
        scratch_shapes=[
            pltpu.VMEM((blocks, 128, 2 * BLOCK), BF16),
            pltpu.VMEM((blocks, BLOCK, 128), BF16),
            pltpu.VMEM((blocks + 1, 64 + ONES, BLOCK), BF16),
            pltpu.VMEM((ITEMS, GROUP * BLOCK, 2 * BLOCK), F32),
            pltpu.VMEM((ITEMS, GROUP * BLOCK, 2 * BLOCK), BF16),
            pltpu.VMEM((ITEMS, 8, 2 * BLOCK), F32),
            pltpu.VMEM((ITEMS, 8, 2 * BLOCK), F32),
            pltpu.VMEM((64 + ONES, 2 * BLOCK), F32),
        ],
        compiler_params=pltpu.CompilerParams(vmem_limit_bytes=40 << 20),
        name="attend",
    )(table, got)


def hand_out_kernel(turned_ref, served_ref, own_ref, mixed_ref, sent_ref, anchor_ref):
    turned = turned_ref[...]
    points = turned.shape[1]
    mixed_ref[...] = flip(turned)
    requests = served_ref.shape[0]

    def picks(rows):
        at = lax.broadcasted_iota(jnp.int32, (points, rows.shape[1]), 0)
        return (at == rows).astype(F32).astype(BF16)

    for r in range(0, requests, 2):
        both = jnp.concatenate([served_ref[r : r + 1, :], served_ref[r + 1 : r + 2, :]], axis=1)
        found = dot(turned, picks(both)).astype(BF16)
        sent_ref[r] = found[:, :BLOCK]
        sent_ref[r + 1] = found[:, BLOCK:]
    anchor_ref[...] = dot(turned, picks(own_ref[...])).astype(BF16)


def hand_out(turned, served, own_rows):
    width, points = turned.shape
    requests, capacity = served.shape
    anchors = own_rows.shape[1]
    return pl.pallas_call(
        hand_out_kernel,
        out_shape=(
            jax.ShapeDtypeStruct((points, width), BF16),
            jax.ShapeDtypeStruct((requests, width, capacity), BF16),
            jax.ShapeDtypeStruct((width, anchors), BF16),
        ),
        in_specs=[pl.BlockSpec(memory_space=pltpu.VMEM)] * 3,
        out_specs=[pl.BlockSpec(memory_space=pltpu.VMEM)] * 3,
        compiler_params=pltpu.CompilerParams(vmem_limit_bytes=40 << 20),
        name="hand_out",
    )(turned, served, own_rows)


def contrast_kernel(
    cand_ref, anchor_ref, weight_ref, slot_ref, live_ref, away_ref, kept_ref, embed, unit, inverse,
    expo, slopes, pulls, own_pulls
):
    pieces, width, capacity = cand_ref.shape
    anchors = anchor_ref.shape[1]
    span = 2 * capacity
    steps = pieces // 2
    turned_weight = flip(weight_ref[...])

    def normalise(rows):
        e = dot(turned_weight, rows)
        inv = lax.rsqrt(jnp.sum(e * e, axis=0, keepdims=True) + 1e-06)
        return e, inv, (e * inv).astype(BF16)

    def back(e, inv, g):
        inner = jnp.sum(e * g, axis=0, keepdims=True)
        return (inv * g - e * (inv * inv * inv * inner)).astype(BF16)

    def rows_of(i):
        return jnp.concatenate([cand_ref[2 * i], cand_ref[2 * i + 1]], axis=1)

    own = anchor_ref[...]
    own_embed, own_inverse, own_unit = normalise(own)
    own_rows = flip(own_unit)

    def column(row):
        return flip(jnp.broadcast_to(row.astype(F32), (128, anchors)))[:, :1]

    slot = column(slot_ref[...])
    live = column(live_ref[...])
    position = lax.broadcasted_iota(jnp.int32, (anchors, span), 1).astype(F32)
    sharpness = 1.0 / SHARPNESS_SCALE

    total = jnp.zeros((anchors, capacity), F32)
    right = jnp.zeros((anchors, capacity), F32)
    def take(i, e):
        at = slice(i * span, (i + 1) * span)
        inv = lax.rsqrt(jnp.sum(e * e, axis=0, keepdims=True) + 1e-06)
        embed[:, at] = e
        unit[:, at] = (e * inv).astype(BF16)
        inverse[:, at] = jnp.broadcast_to(inv, (8, span))

    def judge(i, score, total, right):
        at = slice(i * span, (i + 1) * span)
        hit = position == slot - float(i * span)
        kept = jnp.where(hit, score, 0.0)
        right = right + (kept[:, :capacity] + kept[:, capacity:])
        grown = jnp.exp2(score * (sharpness * LOG2E))
        expo[:, at] = grown
        return total + (grown[:, :capacity] + grown[:, capacity:]), right

    e = dot(turned_weight, rows_of(0))
    for i in range(steps):
        following = dot(turned_weight, rows_of(i + 1)) if i + 1 < steps else None
        take(i, e)
        e = following
        if i > 0:
            score = dot(own_rows, unit[:, (i - 1) * span : i * span])
            total, right = judge(i - 1, score, total, right)
    score = dot(own_rows, unit[:, (steps - 1) * span :])
    total, right = judge(steps - 1, score, total, right)
    total = jnp.sum(total, axis=1, keepdims=True)
    right = jnp.sum(right, axis=1, keepdims=True) * sharpness
    loss = jnp.sum(live * (jnp.log(total) - right), axis=0, keepdims=True)
    count = jnp.sum(live, axis=0, keepdims=True)
    sums = four_rows(loss, count)
    share = live / total * sharpness
    push = live * sharpness

    def slope(i):
        at = slice(i * span, (i + 1) * span)
        hit = position == slot - float(i * span)
        d = (expo[:, at] * share - jnp.where(hit, push, 0.0)).astype(BF16)
        slopes[:, at] = d
        return dot(own_unit, d)

    g = slope(0)
    for i in range(steps):
        at = slice(i * span, (i + 1) * span)
        following = slope(i + 1) if i + 1 < steps else None
        part = dot_nt(unit[:, at], slopes[:, at])
        own_grads = part if i == 0 else own_grads + part
        pulls[:, at] = back(embed[:, at], inverse[0:1, at], g)
        g = following
    own_pulls[...] = back(own_embed, own_inverse, own_grads)
    taken = jnp.concatenate([cand_ref[n] for n in range(pieces)], axis=1)
    ways = kept_ref.shape[0]
    rows = width // ways
    half = width // 2
    core = lax.rem(lax.axis_index("seq"), 2)
    for out_ref, mine in ((away_ref, 1 - core), (kept_ref, core)):
        at = pl.ds(pl.multiple_of(mine * half, half), half)
        grad = dot_nt(taken, pulls[at, :])
        grad = (grad + dot_nt(own, own_pulls[at, :])).astype(BF16)
        for j in range(ways):
            for m in range(half // 128):
                out_ref[j, m * rows : (m + 1) * rows, :] = grad[
                    j * rows : (j + 1) * rows, m * 128 : (m + 1) * 128
                ]
            out_ref[j, rows * half // 128 :, :] = sums


def contrast(candidates, anchors, weight, slot, live, ways):
    pieces, width, capacity = candidates.shape
    count = anchors.shape[1]
    many = pieces * capacity
    half = jax.ShapeDtypeStruct((ways, width * width // 2 // ways // 128 + 8, 128), BF16)
    return pl.pallas_call(
        contrast_kernel,
        out_shape=(half,) * 2,
        in_specs=[pl.BlockSpec(memory_space=pltpu.VMEM)] * 5,
        out_specs=[pl.BlockSpec(memory_space=pltpu.VMEM)] * 2,
        scratch_shapes=[
            pltpu.VMEM((width, many), F32),
            pltpu.VMEM((width, many), BF16),
            pltpu.VMEM((8, many), F32),
            pltpu.VMEM((count, many), F32),
            pltpu.VMEM((count, many), BF16),
            pltpu.VMEM((width, many), BF16),
            pltpu.VMEM((width, count), BF16),
        ],
        compiler_params=pltpu.CompilerParams(vmem_limit_bytes=48 << 20),
        name="contrast",
    )(candidates, anchors, weight, slot, live)


def summed(got_ref):
    total = got_ref[0].astype(F32)
    for n in range(1, got_ref.shape[0]):
        total += got_ref[n].astype(F32)
    part, sums = total[:-8], total[-8:]
    return part, sums[0:1] + sums[2:3], sums[1:2] + sums[3:4]


def first_sum_kernel(got_ref, out_ref):
    part, loss, count = summed(got_ref)
    rows = part.shape[0]
    part = part.astype(BF16)
    sums = four_rows(loss, count)
    for n in range(out_ref.shape[0]):
        out_ref[n, :rows, :] = part
        out_ref[n, rows:, :] = sums


def last_sum_kernel(got_ref, out_ref, loss_ref):
    part, loss, count = summed(got_ref)
    rows = out_ref.shape[1]
    part = part.astype(BF16)
    whole = jnp.concatenate(
        [part[at : at + rows, :] for at in range(0, part.shape[0], rows)], axis=1
    )
    for n in range(out_ref.shape[0]):
        out_ref[n] = whole
    loss_ref[...] = loss / count


def core_sum_kernel(one_ref, two_ref, out_ref):
    rows = out_ref.shape[1] - 8
    total = one_ref[:, :rows, :].astype(F32) + two_ref[:, :rows, :].astype(F32)
    sums = one_ref[0, rows:, :].astype(F32) + two_ref[0, rows:, :].astype(F32)
    sums = four_rows(sums[0:1] + sums[2:3], sums[1:2] + sums[3:4])
    out_ref[:, :rows, :] = total.astype(BF16)
    for n in range(out_ref.shape[0]):
        out_ref[n, rows:, :] = sums


def groups():
    close = lax.axis_size(("view", "seq"))
    events = lax.axis_size("event")
    deep = EVENT_RUN if events % EVENT_RUN == 0 else events
    planes = [
        [
            near * events + far * deep + z
            for near in range(core, close, 2)
            for far in range(events // deep)
        ]
        for core in range(2)
        for z in range(deep)
    ]
    lines = [[far * deep + z for z in range(deep)] for far in range(events // deep)]
    return planes, lines


def to_other_core(x):
    peers = lax.axis_size("seq")
    return lax.ppermute(x, "seq", [(i, i ^ 1) for i in range(peers)])


def small(kernel, name, out_shape, *operands):
    vmem = pl.BlockSpec(memory_space=pltpu.VMEM)
    return pl.pallas_call(
        kernel,
        out_shape=out_shape,
        in_specs=[vmem] * len(operands),
        out_specs=jax.tree.map(lambda shape: vmem, out_shape),
        compiler_params=pltpu.CompilerParams(vmem_limit_bytes=12 << 20),
        name=name,
    )(*operands)


def total_over_devices(away, kept, core, width):
    planes, lines = groups()
    everywhere = ("view", "seq", "event")
    ways, half = len(planes[0]), width // 2
    shape = kept.shape
    parts = small(
        core_sum_kernel, "core_sum", jax.ShapeDtypeStruct(shape, BF16), kept, to_other_core(away)
    )
    got = lax.all_to_all(parts, everywhere, 0, 0, axis_index_groups=planes, tiled=True)
    whole = small(
        first_sum_kernel, "first_sum", jax.ShapeDtypeStruct((len(lines[0]),) + shape[1:], BF16), got
    )
    got = lax.all_to_all(whole, "event", 0, 0, axis_index_groups=lines, tiled=True)
    whole, loss = small(
        last_sum_kernel,
        "last_sum",
        (
            jax.ShapeDtypeStruct((ways, width // ways, half), BF16),
            jax.ShapeDtypeStruct((1, 128), F32),
        ),
        got,
    )
    mine = lax.all_to_all(whole, everywhere, 0, 0, axis_index_groups=planes, tiled=True)
    mine = mine.reshape(width, half)
    other = to_other_core(mine)
    grad = jnp.where(
        core == 0,
        jnp.concatenate([mine, other], axis=1),
        jnp.concatenate([other, mine], axis=1),
    )
    return grad.astype(F32), loss[0, 0]


def per_device(
    query, key, value, pattern, out_weight, served, anchor_rows, positive_slot, anchor_live
):
    points, width = query.shape[2:]
    peers = lax.axis_size("seq")
    rows = pattern.shape[2]
    sent = pack(query[0, 0], key[0, 0], value[0, 0], pattern[0, 0][:, None, :], peers)
    sent, core = lax.optimization_barrier((sent, lax.rem(lax.axis_index("seq"), 2)))
    got = lax.all_to_all(sent, "seq", 0, 0, tiled=True)
    part = 3 * (width // peers)
    table = got[:, part : part + rows, :LIST].astype(jnp.int32).reshape(peers * rows, LIST)
    turned = attend(table, got, peers)
    turned = lax.all_to_all(turned, "seq", 0, 0, tiled=True).reshape(width, points)
    mixed, outgoing, anchors = hand_out(turned, served[0, 0], anchor_rows[0])
    incoming = lax.all_to_all(outgoing, ("view", "seq"), 0, 0, tiled=True)
    ways = len(groups()[0][0])
    away, kept = contrast(
        incoming, anchors, out_weight, positive_slot[0], anchor_live[0], ways
    )
    grad_total, loss = total_over_devices(away, kept, core, width)
    return (mixed[None, None], grad_total, loss)


def solution(mesh):
    placed = (
        P("event", "view", "seq", None),
        P("event", "view", "seq", None),
        P("event", "view", "seq", None),
        P("event", "view", "seq", None),
        P(),
        P("event", "view", "seq", None),
        P("event", "view", "seq"),
        P("event", "view", "seq"),
        P("event", "view", "seq"),
    )
    return jax.shard_map(
        per_device,
        mesh=mesh,
        in_specs=placed,
        out_specs=(P("event", "view", "seq", None), P(), P()),
        check_vma=False,
    )
```

```python
import functools

import jax
import jax.numpy as jnp
from jax import lax
from jax.experimental import pallas as pl
from jax.experimental.pallas import tpu as pltpu
from jax.sharding import PartitionSpec as P

HEADS = 16
BLOCK = 128
SHARPNESS_SCALE = 0.07
GROUP = 2
ITEMS = 8
EXTRA = 8
ONES = 16
EVENT_RUN = 8
LIST = 32
NEGATIVE = -1e30
LOG2E = 1.4426950408889634

F32 = jnp.float32
BF16 = jnp.bfloat16


def dot(a, b):
    return lax.dot_general(a, b, (((1,), (0,)), ((), ())), preferred_element_type=F32)


def dot_nt(a, b):
    return lax.dot_general(a, b, (((1,), (1,)), ((), ())), preferred_element_type=F32)


def flip(x):
    return jnp.transpose(x, (1, 0))


def pack_kernel(
    peers, rows, q_hbm, k_hbm, v_hbm, pattern_hbm, out_ref, q_ref, k_ref, v_ref, pattern_ref, sems
):
    points, full = q_ref.shape
    width = full // peers
    spans = [slice(at, at + BLOCK) for at in range(0, points, BLOCK)]
    copies = [pltpu.make_async_copy(pattern_hbm, pattern_ref, sems.at[0])]
    for n, (source, target) in enumerate(((v_hbm, v_ref), (q_hbm, q_ref), (k_hbm, k_ref))):
        for m, span in enumerate(spans):
            copies.append(
                pltpu.make_async_copy(
                    source.at[span, :], target.at[span, :], sems.at[1 + n * len(spans) + m]
                )
            )
    for copy in copies:
        copy.start()

    copies[0].wait()
    blocks = pattern_ref.shape[2]
    allowed = jnp.concatenate([pattern_ref[r] for r in range(rows)], axis=0)
    allowed = (allowed > 0).astype(F32)
    before = lax.broadcasted_iota(jnp.int32, (blocks, blocks), 0)
    after = lax.broadcasted_iota(jnp.int32, (blocks, blocks), 1)
    rank = dot(allowed.astype(BF16), (before <= after).astype(BF16)) - 1.0
    place = lax.broadcasted_iota(jnp.int32, (LIST, blocks), 0).astype(F32)
    number = lax.broadcasted_iota(jnp.int32, (LIST, blocks), 1).astype(F32)
    lane = lax.broadcasted_iota(jnp.int32, (LIST, 128), 1)
    table = jnp.zeros((LIST, 128), F32)
    for r in range(rows):
        on = allowed[r : r + 1, :]
        count = jnp.sum(on, axis=1, keepdims=True)
        here = jnp.where(place < count, place, 0.0)
        hit = jnp.where(rank[r : r + 1, :] == here, on, 0.0)
        column = jnp.sum(hit * number, axis=1, keepdims=True)
        column = jnp.where(place[:, :1] == float(blocks), count, column)
        table = jnp.where(lane == r, column, table)
    lists = flip(table)[:EXTRA, :].astype(BF16)
    tail = jnp.concatenate(
        [lists, jnp.zeros((EXTRA, 128 - LIST), BF16)]
        + [jnp.zeros((EXTRA, 128), BF16)] * (points // 128 - 1),
        axis=1,
    )
    for j in range(peers):
        out_ref[j, 3 * width : 3 * width + EXTRA, :] = tail

    for n, (at, ref) in enumerate(((2, v_ref), (0, q_ref))):
        for m, span in enumerate(spans):
            copies[1 + n * len(spans) + m].wait()
            turned = flip(ref[span, :])
            for j in range(peers):
                out_ref[j, at * width : (at + 1) * width, span] = turned[
                    j * width : (j + 1) * width, :
                ]
    for m, span in enumerate(spans):
        copies[1 + 2 * len(spans) + m].wait()
        for j in range(peers):
            cols = slice(j * width, (j + 1) * width)
            first = k_ref[span.start : span.start + width, cols]
            second = k_ref[span.start + width : span.stop, cols]
            out_ref[j, width : 2 * width, span] = jnp.concatenate([first, second], axis=1)


def pack(queries, keys, values, pattern, peers):
    points, width = queries.shape
    rows = 3 * (width // peers) + EXTRA
    return pl.pallas_call(
        functools.partial(pack_kernel, peers, pattern.shape[0]),
        out_shape=jax.ShapeDtypeStruct((peers, rows, points), BF16),
        in_specs=[pl.BlockSpec(memory_space=pltpu.HBM)] * 4,
        out_specs=pl.BlockSpec(memory_space=pltpu.VMEM),
        scratch_shapes=[
            pltpu.VMEM((points, width), BF16),
            pltpu.VMEM((points, width), BF16),
            pltpu.VMEM((points, width), BF16),
            pltpu.VMEM(pattern.shape, jnp.int32),
            pltpu.SemaphoreType.DMA((1 + 3 * (points // BLOCK),)),
        ],
        compiler_params=pltpu.CompilerParams(vmem_limit_bytes=16 << 20),
        name="pack_heads",
    )(*(pltpu.with_memory_space_constraint(x, pltpu.HBM) for x in (queries, keys, values, pattern)))


def four_rows(first, second):
    row = lax.broadcasted_iota(jnp.int32, (8, 128), 0)
    value = jnp.where(lax.rem(row, 2) == 0, first, second)
    high = value.astype(BF16).astype(F32)
    return jnp.where(row < 2, high, jnp.where(row < 4, value - high, 0.0)).astype(BF16)


def attend_kernel(
    peers, per_peer, table_ref, got_ref, out_ref, qb, kb, vb, scored, weighed, peak, fade, accum
):
    blocks = peers * per_peer
    head = 32
    factor = head ** (-0.5) * LOG2E
    zero = jnp.zeros((head, BLOCK), BF16)
    ones = (lax.broadcasted_iota(jnp.int32, (ONES, BLOCK), 0) == 0).astype(F32).astype(BF16)

    for j in range(peers):
        for b in range(per_peer):
            block = j * per_peer + b
            span = slice(b * BLOCK, (b + 1) * BLOCK)
            scaled = got_ref[j, 0 : 2 * head, span].astype(F32) * factor
            high = scaled.astype(BF16)
            low = (scaled - high.astype(F32)).astype(BF16)
            left = jnp.concatenate([high[:head], zero, low[:head], zero], axis=0)
            right = jnp.concatenate([zero, high[head:], zero, low[head:]], axis=0)
            qb[block, :, 0:BLOCK] = left
            qb[block, :, BLOCK : 2 * BLOCK] = right
            pair = got_ref[j, 2 * head : 4 * head, span]
            first, second = pair[:, : 2 * head], pair[:, 2 * head :]
            kb[block, : BLOCK // 2, :] = jnp.concatenate([first, first], axis=1)
            kb[block, BLOCK // 2 :, :] = jnp.concatenate([second, second], axis=1)
            vb[block, 0 : 2 * head, :] = got_ref[j, 4 * head : 6 * head, span]
            vb[block, 2 * head : 2 * head + ONES, :] = ones

    vb[blocks, :, :] = jnp.zeros((2 * head + ONES, BLOCK), BF16)
    steps_of = [(table_ref[i, blocks] + GROUP - 1) // GROUP for i in range(blocks)]
    items = functools.reduce(lambda x, y: x + y, steps_of)

    def after(item):
        row, step, real = item
        last = (step + 1) * GROUP >= table_ref[row, blocks]
        end = jnp.logical_and(last, row == blocks - 1)
        return (
            jnp.where(jnp.logical_and(last, row < blocks - 1), row + 1, row),
            jnp.where(end, step, jnp.where(last, 0, step + 1)),
            jnp.where(end, 0, real),
        )

    def turn(t, carry, sums=True, weights=True, scores=True):
        best, at_scores, at_weights, at_sums = carry
        if sums:
            take_sums(at_sums)
        if weights:
            best = take_weights(best, at_weights)
        if not scores:
            return best, at_scores, at_scores, at_weights
        take_scores(at_scores)
        following = [after(at_scores[-1])]
        for n in range(ITEMS - 1):
            following.append(after(following[-1]))
        return best, tuple(following), at_scores, at_weights

    def take_sums(at_sums):
        total = accum[...]
        for n, (row, step, real) in enumerate(at_sums):
            first = step * GROUP
            count = jnp.where(real == 1, table_ref[row, blocks], 0)
            picked = []
            for g in range(GROUP):
                picked.append(vb[jnp.where(first + g < count, table_ref[row, first + g], blocks)])
            added = dot(jnp.concatenate(picked, axis=1), weighed[n])
            total = total * fade[n, 0:1, :] + added
            share = pl.reciprocal(total[2 * head : 2 * head + 1, :])
            j, b = row // per_peer, lax.rem(row, per_peer)
            span = pl.ds(pl.multiple_of(b * BLOCK, BLOCK), BLOCK)
            out_ref[j, 0:head, span] = (total[0:head, 0:BLOCK] * share[:, 0:BLOCK]).astype(BF16)
            out_ref[j, head : 2 * head, span] = (
                total[head : 2 * head, BLOCK : 2 * BLOCK] * share[:, BLOCK : 2 * BLOCK]
            ).astype(BF16)
        accum[...] = total

    def take_weights(best, at_weights):
        for n, (row, step, real) in enumerate(at_weights):
            best = jnp.where(jnp.logical_and(step == 0, real == 1), NEGATIVE, best)
            new_best = jnp.maximum(best, peak[n, 0:1, :])
            weighed[n] = jnp.exp2(scored[n] - new_best).astype(BF16)
            fade[n] = jnp.broadcast_to(jnp.exp2(best - new_best), (8, 2 * BLOCK))
            best = new_best
        return best

    def take_scores(at_scores):
        for n, (row, step, real) in enumerate(at_scores):
            picked = [kb[table_ref[row, step * GROUP + g]] for g in range(GROUP)]
            scores = dot(jnp.concatenate(picked, axis=0), qb[row])
            scored[n] = scores
            top = jnp.max(scores.reshape(GROUP * BLOCK // 8, 8, 2 * BLOCK), axis=0)
            peak[n] = jnp.broadcast_to(jnp.max(top, axis=0, keepdims=True), (8, 2 * BLOCK))

    zero = jnp.int32(0)
    items_at = [(zero, zero, jnp.int32(1))]
    for n in range(ITEMS - 1):
        items_at.append(after(items_at[-1]))
    idle = ((zero, zero, zero),) * ITEMS
    accum[...] = jnp.zeros_like(accum)
    carry = (jnp.full((1, 2 * BLOCK), NEGATIVE, F32), tuple(items_at), idle, idle)
    carry = turn(0, carry, sums=False, weights=False)
    carry = turn(1, carry, sums=False)
    carry = lax.fori_loop(2, (items + ITEMS - 1) // ITEMS, turn, carry)
    carry = turn(0, carry, scores=False)
    turn(0, carry, weights=False, scores=False)


def attend(table, got, peers):
    points = got.shape[2]
    per_peer = points // BLOCK
    blocks = peers * per_peer
    return pl.pallas_call(
        functools.partial(attend_kernel, peers, per_peer),
        out_shape=jax.ShapeDtypeStruct((peers, 64, points), BF16),
        in_specs=[
            pl.BlockSpec(memory_space=pltpu.SMEM),
            pl.BlockSpec(memory_space=pltpu.VMEM),
        ],
        out_specs=pl.BlockSpec(memory_space=pltpu.VMEM),
        scratch_shapes=[
            pltpu.VMEM((blocks, 128, 2 * BLOCK), BF16),
            pltpu.VMEM((blocks, BLOCK, 128), BF16),
            pltpu.VMEM((blocks + 1, 64 + ONES, BLOCK), BF16),
            pltpu.VMEM((ITEMS, GROUP * BLOCK, 2 * BLOCK), F32),
            pltpu.VMEM((ITEMS, GROUP * BLOCK, 2 * BLOCK), BF16),
            pltpu.VMEM((ITEMS, 8, 2 * BLOCK), F32),
            pltpu.VMEM((ITEMS, 8, 2 * BLOCK), F32),
            pltpu.VMEM((64 + ONES, 2 * BLOCK), F32),
        ],
        compiler_params=pltpu.CompilerParams(vmem_limit_bytes=40 << 20),
        name="attend",
    )(table, got)


def hand_out_kernel(turned_ref, served_ref, own_ref, mixed_ref, sent_ref, anchor_ref):
    turned = turned_ref[...]
    points = turned.shape[1]
    mixed_ref[...] = flip(turned)
    requests = served_ref.shape[0]

    def picks(rows):
        at = lax.broadcasted_iota(jnp.int32, (points, rows.shape[1]), 0)
        return (at == rows).astype(F32).astype(BF16)

    for r in range(0, requests, 2):
        both = jnp.concatenate([served_ref[r : r + 1, :], served_ref[r + 1 : r + 2, :]], axis=1)
        found = dot(turned, picks(both)).astype(BF16)
        sent_ref[r] = found[:, :BLOCK]
        sent_ref[r + 1] = found[:, BLOCK:]
    anchor_ref[...] = dot(turned, picks(own_ref[...])).astype(BF16)


def hand_out(turned, served, own_rows):
    width, points = turned.shape
    requests, capacity = served.shape
    anchors = own_rows.shape[1]
    return pl.pallas_call(
        hand_out_kernel,
        out_shape=(
            jax.ShapeDtypeStruct((points, width), BF16),
            jax.ShapeDtypeStruct((requests, width, capacity), BF16),
            jax.ShapeDtypeStruct((width, anchors), BF16),
        ),
        in_specs=[pl.BlockSpec(memory_space=pltpu.VMEM)] * 3,
        out_specs=[pl.BlockSpec(memory_space=pltpu.VMEM)] * 3,
        compiler_params=pltpu.CompilerParams(vmem_limit_bytes=40 << 20),
        name="hand_out",
    )(turned, served, own_rows)


def contrast_kernel(
    cand_ref, anchor_ref, weight_ref, slot_ref, live_ref, away_ref, kept_ref, embed, unit, inverse,
    expo, slopes, pulls, own_pulls
):
    pieces, width, capacity = cand_ref.shape
    anchors = anchor_ref.shape[1]
    span = 2 * capacity
    steps = pieces // 2
    turned_weight = flip(weight_ref[...])

    def normalise(rows):
        e = dot(turned_weight, rows)
        inv = lax.rsqrt(jnp.sum(e * e, axis=0, keepdims=True) + 1e-06)
        return e, inv, (e * inv).astype(BF16)

    def back(e, inv, g):
        inner = jnp.sum(e * g, axis=0, keepdims=True)
        return (inv * g - e * (inv * inv * inv * inner)).astype(BF16)

    def rows_of(i):
        return jnp.concatenate([cand_ref[2 * i], cand_ref[2 * i + 1]], axis=1)

    own = anchor_ref[...]
    own_embed, own_inverse, own_unit = normalise(own)
    own_rows = flip(own_unit)

    def column(row):
        return flip(jnp.broadcast_to(row.astype(F32), (128, anchors)))[:, :1]

    slot = column(slot_ref[...])
    live = column(live_ref[...])
    position = lax.broadcasted_iota(jnp.int32, (anchors, span), 1).astype(F32)
    sharpness = 1.0 / SHARPNESS_SCALE

    total = jnp.zeros((anchors, capacity), F32)
    right = jnp.zeros((anchors, capacity), F32)
    def take(i, e):
        at = slice(i * span, (i + 1) * span)
        inv = lax.rsqrt(jnp.sum(e * e, axis=0, keepdims=True) + 1e-06)
        embed[:, at] = e
        unit[:, at] = (e * inv).astype(BF16)
        inverse[:, at] = jnp.broadcast_to(inv, (8, span))

    def judge(i, score, total, right):
        at = slice(i * span, (i + 1) * span)
        hit = position == slot - float(i * span)
        kept = jnp.where(hit, score, 0.0)
        right = right + (kept[:, :capacity] + kept[:, capacity:])
        grown = jnp.exp2(score * (sharpness * LOG2E))
        expo[:, at] = grown
        return total + (grown[:, :capacity] + grown[:, capacity:]), right

    e = dot(turned_weight, rows_of(0))
    for i in range(steps):
        following = dot(turned_weight, rows_of(i + 1)) if i + 1 < steps else None
        take(i, e)
        e = following
        if i > 0:
            score = dot(own_rows, unit[:, (i - 1) * span : i * span])
            total, right = judge(i - 1, score, total, right)
    score = dot(own_rows, unit[:, (steps - 1) * span :])
    total, right = judge(steps - 1, score, total, right)
    total = jnp.sum(total, axis=1, keepdims=True)
    right = jnp.sum(right, axis=1, keepdims=True) * sharpness
    loss = jnp.sum(live * (jnp.log(total) - right), axis=0, keepdims=True)
    count = jnp.sum(live, axis=0, keepdims=True)
    sums = four_rows(loss, count)
    share = live / total * sharpness
    push = live * sharpness

    def slope(i):
        at = slice(i * span, (i + 1) * span)
        hit = position == slot - float(i * span)
        d = (expo[:, at] * share - jnp.where(hit, push, 0.0)).astype(BF16)
        slopes[:, at] = d
        return dot(own_unit, d)

    g = slope(0)
    for i in range(steps):
        at = slice(i * span, (i + 1) * span)
        following = slope(i + 1) if i + 1 < steps else None
        part = dot_nt(unit[:, at], slopes[:, at])
        own_grads = part if i == 0 else own_grads + part
        pulls[:, at] = back(embed[:, at], inverse[0:1, at], g)
        g = following
    own_pulls[...] = back(own_embed, own_inverse, own_grads)
    taken = jnp.concatenate([cand_ref[n] for n in range(pieces)], axis=1)
    ways = kept_ref.shape[0]
    rows = width // ways
    half = width // 2
    core = lax.rem(lax.axis_index("seq"), 2)
    for out_ref, mine in ((away_ref, 1 - core), (kept_ref, core)):
        at = pl.ds(pl.multiple_of(mine * half, half), half)
        grad = dot_nt(taken, pulls[at, :])
        grad = (grad + dot_nt(own, own_pulls[at, :])).astype(BF16)
        for j in range(ways):
            for m in range(half // 128):
                out_ref[j, m * rows : (m + 1) * rows, :] = grad[
                    j * rows : (j + 1) * rows, m * 128 : (m + 1) * 128
                ]
            out_ref[j, rows * half // 128 :, :] = sums


def contrast(candidates, anchors, weight, slot, live, ways):
    pieces, width, capacity = candidates.shape
    count = anchors.shape[1]
    many = pieces * capacity
    half = jax.ShapeDtypeStruct((ways, width * width // 2 // ways // 128 + 8, 128), BF16)
    return pl.pallas_call(
        contrast_kernel,
        out_shape=(half,) * 2,
        in_specs=[pl.BlockSpec(memory_space=pltpu.VMEM)] * 5,
        out_specs=[pl.BlockSpec(memory_space=pltpu.VMEM)] * 2,
        scratch_shapes=[
            pltpu.VMEM((width, many), F32),
            pltpu.VMEM((width, many), BF16),
            pltpu.VMEM((8, many), F32),
            pltpu.VMEM((count, many), F32),
            pltpu.VMEM((count, many), BF16),
            pltpu.VMEM((width, many), BF16),
            pltpu.VMEM((width, count), BF16),
        ],
        compiler_params=pltpu.CompilerParams(vmem_limit_bytes=48 << 20),
        name="contrast",
    )(candidates, anchors, weight, slot, live)


def summed(got_ref):
    total = got_ref[0].astype(F32)
    for n in range(1, got_ref.shape[0]):
        total += got_ref[n].astype(F32)
    part, sums = total[:-8], total[-8:]
    return part, sums[0:1] + sums[2:3], sums[1:2] + sums[3:4]


def first_sum_kernel(got_ref, out_ref):
    part, loss, count = summed(got_ref)
    rows = part.shape[0]
    part = part.astype(BF16)
    sums = four_rows(loss, count)
    for n in range(out_ref.shape[0]):
        out_ref[n, :rows, :] = part
        out_ref[n, rows:, :] = sums


def last_sum_kernel(got_ref, out_ref, loss_ref):
    part, loss, count = summed(got_ref)
    rows = out_ref.shape[0]
    part = part.astype(BF16)
    out_ref[...] = jnp.concatenate(
        [part[at : at + rows, :] for at in range(0, part.shape[0], rows)], axis=1
    )
    loss_ref[...] = loss / count


def join_kernel(mine_ref, other_ref, out_ref):
    core = lax.rem(lax.axis_index("seq"), 2)
    half = mine_ref.shape[1]
    mine, other = mine_ref[...], other_ref[...]
    first = jnp.where(core == 0, mine, other)
    second = jnp.where(core == 0, other, mine)
    for n in range(out_ref.shape[0]):
        out_ref[n, :, :half] = first
        out_ref[n, :, half:] = second


def core_sum_kernel(one_ref, two_ref, out_ref):
    rows = out_ref.shape[1] - 8
    total = one_ref[:, :rows, :].astype(F32) + two_ref[:, :rows, :].astype(F32)
    sums = one_ref[0, rows:, :].astype(F32) + two_ref[0, rows:, :].astype(F32)
    sums = four_rows(sums[0:1] + sums[2:3], sums[1:2] + sums[3:4])
    out_ref[:, :rows, :] = total.astype(BF16)
    for n in range(out_ref.shape[0]):
        out_ref[n, rows:, :] = sums


def groups():
    close = lax.axis_size(("view", "seq"))
    events = lax.axis_size("event")
    deep = EVENT_RUN if events % EVENT_RUN == 0 else events
    planes = [
        [
            near * events + far * deep + z
            for near in range(core, close, 2)
            for far in range(events // deep)
        ]
        for core in range(2)
        for z in range(deep)
    ]
    lines = [[far * deep + z for z in range(deep)] for far in range(events // deep)]
    return planes, lines


def to_other_core(x):
    peers = lax.axis_size("seq")
    return lax.ppermute(x, "seq", [(i, i ^ 1) for i in range(peers)])


def small(kernel, name, out_shape, *operands):
    vmem = pl.BlockSpec(memory_space=pltpu.VMEM)
    return pl.pallas_call(
        kernel,
        out_shape=out_shape,
        in_specs=[vmem] * len(operands),
        out_specs=jax.tree.map(lambda shape: vmem, out_shape),
        compiler_params=pltpu.CompilerParams(vmem_limit_bytes=12 << 20),
        name=name,
    )(*operands)


def total_over_devices(away, kept, width):
    planes, lines = groups()
    everywhere = ("view", "seq", "event")
    ways, half = len(planes[0]), width // 2
    shape = kept.shape
    parts = small(
        core_sum_kernel, "core_sum", jax.ShapeDtypeStruct(shape, BF16), kept, to_other_core(away)
    )
    got = lax.all_to_all(parts, everywhere, 0, 0, axis_index_groups=planes, tiled=True)
    whole = small(
        first_sum_kernel, "first_sum", jax.ShapeDtypeStruct((len(lines[0]),) + shape[1:], BF16), got
    )
    got = lax.all_to_all(whole, "event", 0, 0, axis_index_groups=lines, tiled=True)
    mine, loss = small(
        last_sum_kernel,
        "last_sum",
        (
            jax.ShapeDtypeStruct((width // ways, half), BF16),
            jax.ShapeDtypeStruct((1, 128), F32),
        ),
        got,
    )
    whole = small(
        join_kernel,
        "join",
        jax.ShapeDtypeStruct((ways, width // ways, width), BF16),
        mine,
        to_other_core(mine),
    )
    grad = lax.all_to_all(whole, everywhere, 0, 0, axis_index_groups=planes, tiled=True)
    grad = grad.reshape(width, width)
    return grad.astype(F32), loss[0, 0]


def per_device(
    query, key, value, pattern, out_weight, served, anchor_rows, positive_slot, anchor_live
):
    points, width = query.shape[2:]
    peers = lax.axis_size("seq")
    rows = pattern.shape[2]
    sent = pack(query[0, 0], key[0, 0], value[0, 0], pattern[0, 0][:, None, :], peers)
    got = lax.all_to_all(sent, "seq", 0, 0, tiled=True)
    part = 3 * (width // peers)
    table = got[:, part : part + rows, :LIST].astype(jnp.int32).reshape(peers * rows, LIST)
    turned = attend(table, got, peers)
    turned = lax.all_to_all(turned, "seq", 0, 0, tiled=True).reshape(width, points)
    mixed, outgoing, anchors = hand_out(turned, served[0, 0], anchor_rows[0])
    incoming = lax.all_to_all(outgoing, ("view", "seq"), 0, 0, tiled=True)
    ways = len(groups()[0][0])
    away, kept = contrast(
        incoming, anchors, out_weight, positive_slot[0], anchor_live[0], ways
    )
    grad_total, loss = total_over_devices(away, kept, width)
    return (mixed[None, None], grad_total, loss)


def solution(mesh):
    placed = (
        P("event", "view", "seq", None),
        P("event", "view", "seq", None),
        P("event", "view", "seq", None),
        P("event", "view", "seq", None),
        P(),
        P("event", "view", "seq", None),
        P("event", "view", "seq"),
        P("event", "view", "seq"),
        P("event", "view", "seq"),
    )
    return jax.shard_map(
        per_device,
        mesh=mesh,
        in_specs=placed,
        out_specs=(P("event", "view", "seq", None), P(), P()),
        check_vma=False,
    )
```
